32 devices in a mesh: feed: 8 (over z, x), tm: 4 (over y, core).
Axes of the slice: x: 2, y: 2, z: 4, core: 2. Of those that a mesh axis runs over, the one named last changes fastest.
Arguments:
- voltages: bfloat16 [2048, 131072], P('feed', 'tm'), may hold values from -6 to 6
- feed_slot: int32 [2048], replicated, may hold values from 0 to 2047, each once
- channel_flags: int32 [1024], replicated, may hold values from 0 to 1, as said below
Outputs:
- beam_power: float32 [96, 16, 1024], P(('feed', 'tm'))
The draws below stay inside these ranges and needn't reach their ends.
Inputs may be any that keep to these rules, and one draw needn't show every extreme that they name: `channel_flags`: exactly 96 entries are 1. `feed_slot`: each slot is named by exactly one input.
All inputs are finite; a program needn't handle non-finite values.
Results may differ from the reference program's by a relative error of at most 0.01.
Values may be sent and summed in bfloat16 or wider, within the bound.
A program may use at most 128 MiB of HBM per device.

```python
import math
import jax
import jax.numpy as jnp
from jax import lax

CHANNELS = 1024
TAPS = 4
CYL = 4
NS = 256
UPCH = 16
FRAME = 2048
INPUTS = 2048
FR_DEV = 16
IN_DEV = 256
LIVE = 96
N_TM = 4


def draw_channel_flags(key, part):
    shuffled = jax.random.permutation(jax.random.fold_in(key, 11), CHANNELS)
    return (shuffled < LIVE).astype(jnp.int32)


def shard_levels(rng, shape, split, least, top_value):
    def one(position, parts):
        heights = jax.random.uniform(jax.random.fold_in(jax.random.fold_in(rng, 6), position), (parts,), jnp.float32, least / len(split), top_value / len(split))
        return jnp.repeat(jnp.exp(heights), shape[position] // parts).reshape((-1,) + (1,) * (len(shape) - position - 1))

    level = one(*split[0])
    for cut in split[1:]:
        level = level * one(*cut)
    return level


def normal_values(own_key, extent, width, reach, shards=(), kind=jnp.bfloat16):
    gain = shard_levels(own_key, extent, shards, -0.22, 0.18) if shards else 1.0
    entries = jax.random.normal(own_key, extent, jnp.float32) * width * gain
    return jnp.minimum(jnp.maximum(entries, -reach), reach).astype(kind)


def setup_inputs(seed: int = 0) -> dict:
    keys = jax.random.split(jax.random.key(seed), 4)
    return {
        "voltages": normal_values(keys[0], (INPUTS, N_TM * FR_DEV * FRAME), 1.0, 6.0, ((0, 8), (1, 4))),
        "feed_slot": jax.random.permutation(keys[1], INPUTS).astype(jnp.int32),
        "channel_flags": draw_channel_flags(jax.random.fold_in(keys[3], 71), 0),
    }


def pfb_window():
    length = TAPS * 2 * CHANNELS
    sample = jnp.arange(length, dtype=jnp.float32)
    offset = (sample - length / 2 + 0.5) / (2 * CHANNELS)
    taper = 0.5 - 0.5 * jnp.cos(2.0 * jnp.pi * (sample + 0.5) / length)
    return (jnp.sinc(offset) * taper).reshape(TAPS, 2 * CHANNELS)

def phase_pair(modulus, first, second, scale):
    product = jnp.arange(first, dtype=jnp.int32)[:, None] * jnp.arange(second, dtype=jnp.int32)[None, :] % modulus
    angle = product.astype(jnp.float32) * (2.0 * jnp.pi / modulus)
    return (jnp.cos(angle) * scale, jnp.sin(angle) * scale)

def channel_table():
    cosine, sine = phase_pair(2 * CHANNELS, CHANNELS, 2 * CHANNELS, 1.0 / math.sqrt(2 * CHANNELS))
    return jnp.stack([cosine, -sine]).astype(jnp.bfloat16)

def grid_table():
    cosine, sine = phase_pair(NS, NS, NS, 1.0 / math.sqrt(NS))
    cosine = cosine.astype(jnp.bfloat16)
    sine = sine.astype(jnp.bfloat16)
    return jnp.stack([jnp.stack([cosine, -sine], axis=1), jnp.stack([sine, cosine], axis=1)])

def pfb_filter(extended, n_frames):
    window = pfb_window()
    summed = jnp.zeros((extended.shape[0], n_frames, extended.shape[2]), jnp.float32)
    for tap_index in range(TAPS):
        summed = summed + window[tap_index] * extended[:, tap_index:tap_index + n_frames].astype(jnp.float32)
    return summed.astype(jnp.bfloat16)

def beamform(spectra, inverse):
    highest = lax.Precision.HIGHEST
    chans, frames = (spectra.shape[0], spectra.shape[1])
    cells = jnp.take(spectra, inverse, axis=3).reshape(chans, frames, 2, 2, CYL, NS)
    ns_out = jnp.einsum('cfrpym,rmqn->cfpyqn', cells.astype(jnp.float32), grid_table().astype(jnp.float32), precision=highest)
    real_part = ns_out[:, :, :, :, 0]
    imag_part = ns_out[:, :, :, :, 1]
    ew_cos, ew_sin = phase_pair(CYL, CYL, CYL, 1.0 / math.sqrt(CYL))
    beam_re = jnp.einsum('cfpyn,ye->cfpen', real_part, ew_cos, precision=highest) + jnp.einsum('cfpyn,ye->cfpen', imag_part, ew_sin, precision=highest)
    beam_im = jnp.einsum('cfpyn,ye->cfpen', imag_part, ew_cos, precision=highest) - jnp.einsum('cfpyn,ye->cfpen', real_part, ew_sin, precision=highest)
    return jnp.stack([beam_re, beam_im], axis=2).astype(jnp.bfloat16)

def block_power(beams, blocks):
    highest = lax.Precision.HIGHEST
    chans = beams.shape[0]
    shaped = beams.reshape(chans, blocks, UPCH, 2, 2, CYL, NS).astype(jnp.float32)
    beam_re = shaped[:, :, :, 0]
    beam_im = shaped[:, :, :, 1]
    up_cos, up_sin = phase_pair(UPCH, UPCH, UPCH, 1.0 / math.sqrt(UPCH))
    up_cos = up_cos.astype(jnp.bfloat16).astype(jnp.float32)
    up_sin = up_sin.astype(jnp.bfloat16).astype(jnp.float32)
    up_re = jnp.einsum('cbupen,uk->cbkpen', beam_re, up_cos, precision=highest) + jnp.einsum('cbupen,uk->cbkpen', beam_im, up_sin, precision=highest)
    up_im = jnp.einsum('cbupen,uk->cbkpen', beam_im, up_cos, precision=highest) - jnp.einsum('cbupen,uk->cbkpen', beam_re, up_sin, precision=highest)
    summed = lax.optimization_barrier(jnp.sum(up_re * up_re + up_im * up_im, axis=(1, 3)))
    return summed.reshape(chans, UPCH, CYL * NS)

def reference(voltages, feed_slot, channel_flags):
    frame_len = 2 * CHANNELS
    n_frames = voltages.shape[1] // frame_len
    live_idx = jnp.nonzero(channel_flags, size=LIVE)[0].astype(jnp.int32)
    coeffs = jnp.take(channel_table(), live_idx, axis=1).astype(jnp.float32)

    def spectra_of(row_block):
        padding = jnp.zeros((row_block.shape[0], (TAPS - 1) * frame_len), jnp.bfloat16)
        extended = jnp.concatenate([padding, row_block], axis=1).reshape(row_block.shape[0], n_frames + TAPS - 1, frame_len)
        filtered = pfb_filter(extended, n_frames)
        return jnp.einsum('rcs,ifs->cfri', coeffs, filtered.astype(jnp.float32), precision=lax.Precision.HIGHEST).astype(jnp.bfloat16)
    grouped = voltages.reshape(INPUTS // IN_DEV, IN_DEV, voltages.shape[1])
    spectra = lax.map(spectra_of, grouped)
    spectra = jnp.moveaxis(spectra, 0, 3).reshape(LIVE, n_frames, 2, INPUTS)
    inverse = jnp.argsort(feed_slot).astype(jnp.int32)

    def channel_power(one_channel):
        beams = beamform(one_channel[None], inverse)
        return block_power(beams, n_frames // UPCH)[0]
    power_sum = lax.map(channel_power, spectra)
    return power_sum / (2.0 * (n_frames // UPCH))
```

```python
import math

import jax
import jax.numpy as jnp
from jax import lax
from jax.sharding import PartitionSpec as P

CHANNELS = 1024
TAPS = 4
CYL = 4
NS = 256
UPCH = 16
LIVE_DEV = 3


def passed_along(block, axis, distance):
    devices = range(lax.axis_size(axis))
    route = [(i - distance, i) for i in devices if i - distance in devices]
    return lax.ppermute(block, axis, route)


def pfb_window():
    length = TAPS * 2 * CHANNELS
    sample = jnp.arange(length, dtype=jnp.float32)
    offset = (sample - length / 2 + 0.5) / (2 * CHANNELS)
    taper = 0.5 - 0.5 * jnp.cos(2.0 * jnp.pi * (sample + 0.5) / length)
    return (jnp.sinc(offset) * taper).reshape(TAPS, 2 * CHANNELS)


def phase_pair(modulus, first, second, scale):
    product = first[:, None] * second[None, :] % modulus
    angle = product.astype(jnp.float32) * (2.0 * jnp.pi / modulus)
    return (jnp.cos(angle) * scale, jnp.sin(angle) * scale)


def grid_table():
    index = jnp.arange(NS, dtype=jnp.int32)
    cosine, sine = phase_pair(NS, index, index, 1.0 / math.sqrt(NS))
    cosine = cosine.astype(jnp.bfloat16)
    sine = sine.astype(jnp.bfloat16)
    return cosine, sine


def live_channels(flags, count):
    k = jnp.arange(flags.shape[0], dtype=jnp.int32)
    seen = jnp.sum(jnp.where(k[None, :] <= k[:, None], flags[None, :], 0), axis=1)
    j = jnp.arange(count, dtype=jnp.int32)
    return jnp.sum((seen[None, :] <= j[:, None]).astype(jnp.int32), axis=1)


def pfb_filter(voltages, n_frames, window):
    inputs = voltages.shape[0]
    frames = voltages.reshape(inputs, n_frames, 2 * CHANNELS).astype(jnp.float32)
    padded = jnp.pad(frames, ((0, 0), (TAPS - 1, TAPS - 1), (0, 0)))
    total = n_frames + TAPS - 1
    summed = 0.0
    for tap in range(TAPS):
        summed = summed + window[tap] * padded[:, tap : tap + total]
    return summed.astype(jnp.bfloat16)


def local(voltages, feed_slot, channel_flags):
    n_frames = voltages.shape[1] // (2 * CHANNELS)
    n_time = lax.axis_size("tm")
    n_feed = lax.axis_size("feed")
    inputs = voltages.shape[0]
    live_count = LIVE_DEV * n_feed * n_time
    chans = LIVE_DEV * n_time
    live = live_channels(channel_flags, live_count)
    cosine, sine = phase_pair(
        2 * CHANNELS, live, jnp.arange(2 * CHANNELS, dtype=jnp.int32), 1.0 / math.sqrt(2 * CHANNELS)
    )
    coeffs = jnp.stack([cosine, -sine]).astype(jnp.bfloat16)
    filtered = pfb_filter(voltages, n_frames, pfb_window())
    spectra = jnp.einsum("rcs,ifs->rcfi", coeffs, filtered, preferred_element_type=jnp.float32)
    earlier = passed_along(spectra[:, :, n_frames:].astype(jnp.bfloat16), "tm", 1)
    spectra = spectra[:, :, :n_frames]
    spectra = jnp.concatenate(
        [spectra[:, :, : TAPS - 1] + earlier.astype(jnp.float32), spectra[:, :, TAPS - 1 :]], axis=2
    ).astype(jnp.bfloat16)
    turned = lax.all_to_all(
        spectra.reshape(2, n_feed, chans, n_frames, inputs), "feed", split_axis=1, concat_axis=1, tiled=True
    )
    slots = feed_slot.reshape(n_feed, inputs)
    onehot = (slots[:, :, None] == jnp.arange(n_feed * inputs, dtype=jnp.int32)).astype(jnp.bfloat16)
    cells = jnp.einsum(
        "rscfi,sin->rcfn", turned, onehot, preferred_element_type=jnp.float32
    ).astype(jnp.bfloat16)
    cells = cells.reshape(2, chans, n_frames, 2 * CYL, NS)
    cosine, sine = grid_table()
    table = jnp.stack([jnp.stack([cosine, -sine], axis=1), jnp.stack([sine, cosine], axis=1)])
    ns_out = jnp.einsum("rcfgm,rmqn->qcfgn", cells, table, preferred_element_type=jnp.float32)
    z = ns_out.reshape(2, chans, n_frames, 2, CYL, NS)
    re, im = z[0], z[1]
    r = [re[:, :, :, y] for y in range(CYL)]
    i = [im[:, :, :, y] for y in range(CYL)]
    t0r, t1r, t2r, t3r = r[0] + r[2], r[0] - r[2], r[1] + r[3], r[1] - r[3]
    t0i, t1i, t2i, t3i = i[0] + i[2], i[0] - i[2], i[1] + i[3], i[1] - i[3]
    beam_re = jnp.stack([t0r + t2r, t1r + t3i, t0r - t2r, t1r - t3i], axis=3)
    beam_im = jnp.stack([t0i + t2i, t1i - t3r, t0i - t2i, t1i + t3r], axis=3)
    beams = (jnp.stack([beam_re, beam_im]) * 0.5).astype(jnp.bfloat16)
    blocks = n_frames // UPCH
    beams = beams.reshape(2, chans, blocks, UPCH, 2, CYL * NS)
    index = jnp.arange(UPCH, dtype=jnp.int32)
    up_cos, up_sin = phase_pair(UPCH, index, index, 1.0 / math.sqrt(UPCH))
    up_cos = up_cos.astype(jnp.bfloat16)
    up_sin = up_sin.astype(jnp.bfloat16)
    up_table = jnp.stack([jnp.stack([up_cos, -up_sin], axis=1), jnp.stack([up_sin, up_cos], axis=1)])
    up = jnp.einsum("qcbupn,quvk->vcbkpn", beams, up_table, preferred_element_type=jnp.float32)
    power = jnp.sum(up * up, axis=(0, 2, 4)) * (1.0 / (2.0 * n_time * blocks))
    parts = lax.all_to_all(
        power.astype(jnp.bfloat16).reshape(n_time, LIVE_DEV, UPCH, CYL * NS), "tm", split_axis=0, concat_axis=0, tiled=True
    )
    return jnp.sum(parts.astype(jnp.float32), axis=0)


def solution(mesh):
    in_specs = (P("feed", "tm"), P(), P())
    out_specs = P(("feed", "tm"), None, None)
    return jax.shard_map(local, mesh=mesh, in_specs=in_specs, out_specs=out_specs, check_vma=False)
```

```python
import math

import functools

import jax
import jax.numpy as jnp
from jax import lax
from jax.experimental import pallas as pl
from jax.experimental.pallas import tpu as pltpu
from jax.sharding import PartitionSpec as P

CHANNELS = 1024
TAPS = 4
CYL = 4
NS = 256
UPCH = 16
LIVE_DEV = 3


def passed_along(block, axis, distance):
    devices = range(lax.axis_size(axis))
    route = [(i - distance, i) for i in devices if i - distance in devices]
    return lax.ppermute(block, axis, route)


def pfb_window():
    length = TAPS * 2 * CHANNELS
    sample = jnp.arange(length, dtype=jnp.float32)
    offset = (sample - length / 2 + 0.5) / (2 * CHANNELS)
    taper = 0.5 - 0.5 * jnp.cos(2.0 * jnp.pi * (sample + 0.5) / length)
    return (jnp.sinc(offset) * taper).reshape(TAPS, 2 * CHANNELS)


def phase_pair(modulus, first, second, scale):
    product = first[:, None] * second[None, :] % modulus
    angle = product.astype(jnp.float32) * (2.0 * jnp.pi / modulus)
    return (jnp.cos(angle) * scale, jnp.sin(angle) * scale)


def grid_table():
    index = jnp.arange(NS, dtype=jnp.int32)
    cosine, sine = phase_pair(NS, index, index, 1.0 / math.sqrt(NS))
    cosine = cosine.astype(jnp.bfloat16)
    sine = sine.astype(jnp.bfloat16)
    return cosine, sine


def live_channels(flags, count):
    k = jnp.arange(flags.shape[0], dtype=jnp.int32)
    seen = jnp.sum(jnp.where(k[None, :] <= k[:, None], flags[None, :], 0), axis=1)
    j = jnp.arange(count, dtype=jnp.int32)
    return jnp.sum((seen[None, :] <= j[:, None]).astype(jnp.int32), axis=1)


def pfb_filter(voltages, n_frames, window):
    inputs = voltages.shape[0]
    frames = voltages.reshape(inputs, n_frames, 2 * CHANNELS).astype(jnp.float32)
    padded = jnp.pad(frames, ((0, 0), (TAPS - 1, TAPS - 1), (0, 0)))
    total = n_frames + TAPS - 1
    summed = 0.0
    for tap in range(TAPS):
        summed = summed + window[tap] * padded[:, tap : tap + total]
    return summed.astype(jnp.bfloat16)


def local_plain(voltages, feed_slot, channel_flags):
    n_frames = voltages.shape[1] // (2 * CHANNELS)
    n_time = lax.axis_size("tm")
    n_feed = lax.axis_size("feed")
    inputs = voltages.shape[0]
    live_count = LIVE_DEV * n_feed * n_time
    chans = LIVE_DEV * n_time
    live = live_channels(channel_flags, live_count)
    cosine, sine = phase_pair(
        2 * CHANNELS, live, jnp.arange(2 * CHANNELS, dtype=jnp.int32), 1.0 / math.sqrt(2 * CHANNELS)
    )
    coeffs = jnp.stack([cosine, -sine]).astype(jnp.bfloat16)
    filtered = pfb_filter(voltages, n_frames, pfb_window())
    spectra = jnp.einsum("rcs,ifs->rcfi", coeffs, filtered, preferred_element_type=jnp.float32)
    earlier = passed_along(spectra[:, :, n_frames:].astype(jnp.bfloat16), "tm", 1)
    spectra = spectra[:, :, :n_frames]
    spectra = jnp.concatenate(
        [spectra[:, :, : TAPS - 1] + earlier.astype(jnp.float32), spectra[:, :, TAPS - 1 :]], axis=2
    ).astype(jnp.bfloat16)
    turned = lax.all_to_all(
        spectra.reshape(2, n_feed, chans, n_frames, inputs), "feed", split_axis=1, concat_axis=1, tiled=True
    )
    slots = feed_slot.reshape(n_feed, inputs)
    onehot = (slots[:, :, None] == jnp.arange(n_feed * inputs, dtype=jnp.int32)).astype(jnp.bfloat16)
    cells = jnp.einsum(
        "rscfi,sin->rcfn", turned, onehot, preferred_element_type=jnp.float32
    ).astype(jnp.bfloat16)
    cells = cells.reshape(2, chans, n_frames, 2 * CYL, NS)
    cosine, sine = grid_table()
    table = jnp.stack([jnp.stack([cosine, -sine], axis=1), jnp.stack([sine, cosine], axis=1)])
    ns_out = jnp.einsum("rcfgm,rmqn->qcfgn", cells, table, preferred_element_type=jnp.float32)
    z = ns_out.reshape(2, chans, n_frames, 2, CYL, NS)
    re, im = z[0], z[1]
    r = [re[:, :, :, y] for y in range(CYL)]
    i = [im[:, :, :, y] for y in range(CYL)]
    t0r, t1r, t2r, t3r = r[0] + r[2], r[0] - r[2], r[1] + r[3], r[1] - r[3]
    t0i, t1i, t2i, t3i = i[0] + i[2], i[0] - i[2], i[1] + i[3], i[1] - i[3]
    beam_re = jnp.stack([t0r + t2r, t1r + t3i, t0r - t2r, t1r - t3i], axis=3)
    beam_im = jnp.stack([t0i + t2i, t1i - t3r, t0i - t2i, t1i + t3r], axis=3)
    beams = (jnp.stack([beam_re, beam_im]) * 0.5).astype(jnp.bfloat16)
    blocks = n_frames // UPCH
    beams = beams.reshape(2, chans, blocks, UPCH, 2, CYL * NS)
    index = jnp.arange(UPCH, dtype=jnp.int32)
    up_cos, up_sin = phase_pair(UPCH, index, index, 1.0 / math.sqrt(UPCH))
    up_cos = up_cos.astype(jnp.bfloat16)
    up_sin = up_sin.astype(jnp.bfloat16)
    up_table = jnp.stack([jnp.stack([up_cos, -up_sin], axis=1), jnp.stack([up_sin, up_cos], axis=1)])
    up = jnp.einsum("qcbupn,quvk->vcbkpn", beams, up_table, preferred_element_type=jnp.float32)
    power = jnp.sum(up * up, axis=(0, 2, 4)) * (1.0 / (2.0 * n_time * blocks))
    parts = lax.all_to_all(
        power.astype(jnp.bfloat16).reshape(n_time, LIVE_DEV, UPCH, CYL * NS), "tm", split_axis=0, concat_axis=0, tiled=True
    )
    return jnp.sum(parts.astype(jnp.float32), axis=0)


MESH = pl.DeviceIdType.MESH
NT = (((1,), (1,)), ((), ()))


def fused_kernel(
    n_feed, n_time, n_frames, scale,
    volt, coeffs, window, slots, t1, t2, upm, out,
    vp, filt, tmp, send, recv, hist_out, hist_in, onehot, acc, cells, beams, power, psend, precv,
    load_sem, own_sem, hist_sem, send_sem, recv_sem, psend_sem, precv_sem,
):
    me = lax.axis_index("feed")
    tm = lax.axis_index("tm")
    frame = 2 * CHANNELS
    past = TAPS - 1
    quads = n_frames // 4
    inputs = volt.shape[0]
    rows = coeffs.shape[0]
    own_rows = LIVE_DEV * UPCH

    def load(f):
        return pltpu.make_async_copy(
            volt.at[:, f * frame : (f + 1) * frame], vp.at[f + past], load_sem.at[f]
        )

    order = list(range(n_frames - past, n_frames)) + list(range(1, n_frames - past)) + [0]
    for f in order:
        load(f).start()
    barrier = pltpu.get_barrier_semaphore()
    for o in range(1, n_feed):
        pl.semaphore_signal(barrier, inc=1, device_id={"feed": lax.rem(me + o, n_feed)}, device_id_type=MESH)
    for o in range(1, n_time):
        pl.semaphore_signal(barrier, inc=1, device_id={"tm": lax.rem(tm + o, n_time)}, device_id_type=MESH)
    pl.semaphore_wait(barrier, n_feed - 1 + n_time - 1)

    for t in range(past):
        vp[t] = jnp.zeros_like(vp[t])
        vp[n_frames + past + t] = jnp.zeros_like(vp[t])

    def spectra(f):
        width = 256

        def chunk(c, _):
            lanes = pl.ds(pl.multiple_of(c * width, width), width)
            total = window[0:1, lanes] * vp[f, :, lanes].astype(jnp.float32)
            for t in range(1, TAPS):
                total = total + window[t : t + 1, lanes] * vp[f + t, :, lanes].astype(jnp.float32)
            filt[:, lanes] = total.astype(jnp.bfloat16)
            return 0

        lax.fori_loop(0, frame // width, chunk, 0)
        return lax.dot_general(coeffs[...], filt[...], NT, preferred_element_type=jnp.float32)

    for f in range(n_frames - past, n_frames):
        load(f).wait()

    def tail_frame(k, _):
        hist_out[k] = spectra(n_frames + k).astype(jnp.bfloat16)
        return 0

    lax.fori_loop(0, past, tail_frame, 0)

    def hist_copy(to):
        return pltpu.make_async_remote_copy(
            src_ref=hist_out, dst_ref=hist_in, send_sem=hist_sem.at[0], recv_sem=hist_sem.at[1],
            device_id={"tm": to}, device_id_type=MESH,
        )

    @pl.when(tm < n_time - 1)
    def _():
        hist_copy(lax.rem(tm + 1, n_time)).start()

    def send_copy(q, o):
        to = lax.rem(me + o, n_feed)
        return pltpu.make_async_remote_copy(
            src_ref=send.at[q, to], dst_ref=recv.at[me, :, q],
            send_sem=send_sem.at[q, o], recv_sem=recv_sem.at[q, o],
            device_id={"feed": to}, device_id_type=MESH,
        )

    def arrival(q, o):
        back = lax.rem(me + n_feed - o, n_feed)
        return pltpu.make_async_remote_copy(
            src_ref=send.at[q, back], dst_ref=recv.at[back, :, q],
            send_sem=send_sem.at[q, o], recv_sem=recv_sem.at[q, o],
            device_id={"feed": back}, device_id_type=MESH,
        )

    def own_copy(q):
        return pltpu.make_async_copy(send.at[q, me], recv.at[me, :, q], own_sem.at[q])

    def far_first(k):
        return lax.rem(k + n_feed // 2 - 1, n_feed - 1) + 1

    lower = lax.broadcasted_iota(jnp.int32, (8, inputs), 0) < 4

    def quad(q, first):
        def one(k, _):
            value = spectra(q * 4 + k)
            if first:
                value = value + jnp.where(k < past, 1.0, 0.0) * hist_in[jnp.minimum(k, past - 1)].astype(jnp.float32)
            tmp[k] = value
            return 0

        lax.fori_loop(0, 4, one, 0)

        def pack(d, _):
            parts = [[], []]
            at = pl.multiple_of(d * 24, 8)
            for pair in range(2):
                a0, b0, c0 = (tmp[2 * pair, pl.ds(at + 8 * k, 8)] for k in range(3))
                a1, b1, c1 = (tmp[2 * pair + 1, pl.ds(at + 8 * k, 8)] for k in range(3))
                parts[0] += [a0, a1, jnp.where(lower, b0, pltpu.roll(b1, 4, 0))]
                parts[1] += [c0, c1, jnp.where(lower, pltpu.roll(b0, 4, 0), b1)]
            send[q, d, 0] = jnp.concatenate(parts[0], axis=0).astype(jnp.bfloat16)
            send[q, d, 1] = jnp.concatenate(parts[1], axis=0).astype(jnp.bfloat16)
            return 0

        lax.fori_loop(0, n_feed, pack, 0)

        def start(k, _):
            send_copy(q, far_first(k)).start()
            return 0

        lax.fori_loop(0, n_feed - 1, start, 0)
        own_copy(q).start()

    for f in range(1, 4):
        load(f).wait()
    for q in range(1, quads):
        for f in range(4 * q, min(4 * q + 4, n_frames - past)):
            load(f).wait()
        quad(q, False)
    load(0).wait()

    @pl.when(tm > 0)
    def _():
        hist_copy(lax.rem(tm + n_time - 1, n_time)).wait_recv()

    @pl.when(tm == 0)
    def _():
        hist_in[...] = jnp.zeros_like(hist_in)

    quad(0, True)

    total = n_feed * inputs
    which = lax.broadcasted_iota(jnp.int32, (total, inputs), 0)

    def ones(s, _):
        onehot[s] = jnp.where(which == slots[s], 1.0, 0.0).astype(jnp.bfloat16)
        return 0

    lax.fori_loop(0, n_feed, ones, 0)

    step = 512

    def place(s, fresh):
        block = recv[s].reshape(2 * quads * 48, inputs)

        def part(n, _):
            at = pl.multiple_of(n * step, step)
            got = lax.dot_general(block, onehot[s, pl.ds(at, step), :], NT, preferred_element_type=jnp.float32)
            if fresh:
                acc[:, pl.ds(at, step)] = got
            else:
                acc[:, pl.ds(at, step)] += got
            return 0

        lax.fori_loop(0, total // step, part, 0)

    for q in range(quads):
        own_copy(q).wait()
    place(me, True)

    def source(k, _):
        o = lax.rem(k, n_feed - 1) + 1
        for q in range(quads):
            arrival(q, o).wait_recv()
        place(lax.rem(me + n_feed - o, n_feed), False)
        return 0

    lax.fori_loop(0, n_feed - 1, source, 0)
    half = quads * 48
    cells[...] = acc[...].astype(jnp.bfloat16)

    for p in range(2):
        z = []
        for y in range(CYL):
            at = (p * CYL + y) * NS
            value = jnp.dot(cells[:half, at : at + NS], t1[...], preferred_element_type=jnp.float32)
            value = value + jnp.dot(cells[half:, at : at + NS], t2[...], preferred_element_type=jnp.float32)
            z.append((value[:, :NS], value[:, NS:]))
        (r0, i0), (r1, i1), (r2, i2), (r3, i3) = z
        t0r, t1r, t2r, t3r = r0 + r2, r0 - r2, r1 + r3, r1 - r3
        t0i, t1i, t2i, t3i = i0 + i2, i0 - i2, i1 + i3, i1 - i3
        re = [t0r + t2r, t1r + t3i, t0r - t2r, t1r - t3i]
        im = [t0i + t2i, t1i - t3r, t0i - t2i, t1i + t3r]
        for e in range(CYL):
            at = (p * CYL + e) * NS
            beams[:half, at : at + NS] = (re[e] * 0.5).astype(jnp.bfloat16)
            beams[half:, at : at + NS] = (im[e] * 0.5).astype(jnp.bfloat16)

    outs = upm.shape[0] // 2
    for e in range(CYL):
        summed = 0.0
        for p in range(2):
            at = (p * CYL + e) * NS
            up = jnp.dot(upm[...], beams[:, at : at + NS], preferred_element_type=jnp.float32)
            summed = summed + up[:outs] * up[:outs] + up[outs:] * up[outs:]
        summed = summed * scale
        for t in range(n_time):
            block = summed[t * own_rows : (t + 1) * own_rows]
            power[t, :, e * NS : (e + 1) * NS] = block
            psend[t, :, e * NS : (e + 1) * NS] = block.astype(jnp.bfloat16)

    def power_copy(o):
        to = lax.rem(tm + o, n_time)
        return pltpu.make_async_remote_copy(
            src_ref=psend.at[to], dst_ref=precv.at[o - 1],
            send_sem=psend_sem.at[o - 1], recv_sem=precv_sem.at[o - 1],
            device_id={"tm": to}, device_id_type=MESH,
        )

    for o in range(1, n_time):
        power_copy(o).start()
    result = power[tm]
    for o in range(1, n_time):
        power_copy(o).wait_recv()
        result = result + precv[o - 1].astype(jnp.float32)
    out[...] = result
    for o in range(1, n_time):
        power_copy(o).wait_send()

    def drain(k, _):
        for q in range(quads):
            send_copy(q, k + 1).wait_send()
        return 0

    lax.fori_loop(0, n_feed - 1, drain, 0)

    @pl.when(tm < n_time - 1)
    def _():
        hist_copy(lax.rem(tm + 1, n_time)).wait_send()


def row_order(quads):
    frames, chans = [], []
    for q in range(quads):
        for pair in range(2):
            f = 4 * q + 2 * pair
            frames += [f] * 8 + [f + 1] * 8 + [f] * 4 + [f + 1] * 4
            chans += list(range(8)) * 2 + list(range(8, 12)) * 2
    return jnp.array(frames, jnp.int32), jnp.array(chans, jnp.int32)


def local_fused(voltages, feed_slot, channel_flags):
    bf16 = jnp.bfloat16
    frame = 2 * CHANNELS
    inputs = voltages.shape[0]
    n_frames = voltages.shape[1] // frame
    n_time = lax.axis_size("tm")
    n_feed = lax.axis_size("feed")
    chans = LIVE_DEV * n_time
    quads = n_frames // 4
    live = live_channels(channel_flags, chans * n_feed).reshape(n_feed, chans)
    row_chan = jnp.concatenate([live, live[:, 8:], live[:, :8]], axis=1).reshape(-1)
    is_imag = jnp.tile(jnp.arange(2 * chans) >= chans, n_feed)
    product = row_chan[:, None] * jnp.arange(frame, dtype=jnp.int32)[None, :] % frame
    angle = product.astype(jnp.float32) * (2.0 * jnp.pi / frame)
    coeffs = jnp.where(is_imag[:, None], -jnp.sin(angle), jnp.cos(angle)) * (1.0 / math.sqrt(frame))
    coeffs = coeffs.astype(bf16)
    c, d = grid_table()
    t1 = jnp.concatenate([c, -d], axis=1)
    t2 = jnp.concatenate([d, c], axis=1)
    index = jnp.arange(UPCH, dtype=jnp.int32)
    frames, row_ch = row_order(quads)
    up_cos, up_sin = phase_pair(UPCH, index, frames, 1.0 / math.sqrt(UPCH))
    same = (jnp.arange(chans)[:, None] == row_ch[None, :])[:, None, :]
    cm = jnp.where(same, up_cos[None], 0.0).reshape(chans * UPCH, -1)
    sm = jnp.where(same, up_sin[None], 0.0).reshape(chans * UPCH, -1)
    upm = jnp.concatenate([jnp.concatenate([cm, sm], 1), jnp.concatenate([-sm, cm], 1)], 0).astype(bf16)
    rows = 2 * chans * n_feed
    total = n_feed * inputs
    own_rows = LIVE_DEV * UPCH
    half = quads * 48
    vmem = pl.BlockSpec(memory_space=pltpu.VMEM)
    dma = pltpu.SemaphoreType.DMA
    result = pl.pallas_call(
        functools.partial(fused_kernel, n_feed, n_time, n_frames, 1.0 / (2.0 * n_time)),
        out_shape=jax.ShapeDtypeStruct((own_rows, CYL * NS), jnp.float32),
        in_specs=[pl.BlockSpec(memory_space=pl.ANY)] + [vmem] * 6,
        out_specs=vmem,
        scratch_shapes=[
            pltpu.VMEM((n_frames + 2 * TAPS - 2, inputs, frame), bf16),
            pltpu.VMEM((inputs, frame), bf16),
            pltpu.VMEM((4, rows, inputs), jnp.float32),
            pltpu.VMEM((quads, n_feed, 2, 48, inputs), bf16),
            pltpu.VMEM((n_feed, 2, quads, 48, inputs), bf16),
            pltpu.VMEM((TAPS - 1, rows, inputs), bf16),
            pltpu.VMEM((TAPS - 1, rows, inputs), bf16),
            pltpu.VMEM((n_feed, total, inputs), bf16),
            pltpu.VMEM((2 * half, total), jnp.float32),
            pltpu.VMEM((2 * half, total), bf16),
            pltpu.VMEM((2 * half, total), bf16),
            pltpu.VMEM((n_time, own_rows, CYL * NS), jnp.float32),
            pltpu.VMEM((n_time, own_rows, CYL * NS), bf16),
            pltpu.VMEM((n_time - 1, own_rows, CYL * NS), bf16),
            dma((n_frames,)),
            dma((quads,)),
            dma((2,)),
            dma((quads, n_feed)),
            dma((quads, n_feed)),
            dma((n_time - 1,)),
            dma((n_time - 1,)),
        ],
        compiler_params=pltpu.CompilerParams(
            collective_id=0, has_side_effects=True, vmem_limit_bytes=62 * 1024 * 1024
        ),
    )(voltages, coeffs, pfb_window(), feed_slot.reshape(n_feed, 1, inputs), t1, t2, upm)
    return result.reshape(LIVE_DEV, UPCH, CYL * NS)


def local(voltages, feed_slot, channel_flags):
    fits = (
        voltages.shape[0] == NS
        and voltages.shape[1] == UPCH * 2 * CHANNELS
        and lax.axis_size("tm") == 4
        and lax.axis_size("feed") * voltages.shape[0] == 2 * CYL * NS
    )
    return (local_fused if fits else local_plain)(voltages, feed_slot, channel_flags)


def solution(mesh):
    in_specs = (P("feed", "tm"), P(), P())
    out_specs = P(("feed", "tm"), None, None)
    return jax.shard_map(local, mesh=mesh, in_specs=in_specs, out_specs=out_specs, check_vma=False)
```

```python
import math

import functools

import jax
import jax.numpy as jnp
import numpy as np
from jax import lax
from jax.experimental import pallas as pl
from jax.experimental.pallas import tpu as pltpu
from jax.sharding import PartitionSpec as P

CHANNELS = 1024
TAPS = 4
CYL = 4
NS = 256
UPCH = 16
LIVE_DEV = 3


def passed_along(block, axis, distance):
    devices = range(lax.axis_size(axis))
    route = [(i - distance, i) for i in devices if i - distance in devices]
    return lax.ppermute(block, axis, route)


def pfb_window():
    length = TAPS * 2 * CHANNELS
    sample = jnp.arange(length, dtype=jnp.float32)
    offset = (sample - length / 2 + 0.5) / (2 * CHANNELS)
    taper = 0.5 - 0.5 * jnp.cos(2.0 * jnp.pi * (sample + 0.5) / length)
    return (jnp.sinc(offset) * taper).reshape(TAPS, 2 * CHANNELS)


def phase_pair(modulus, first, second, scale):
    product = first[:, None] * second[None, :] % modulus
    angle = product.astype(jnp.float32) * (2.0 * jnp.pi / modulus)
    return (jnp.cos(angle) * scale, jnp.sin(angle) * scale)


def grid_table():
    index = jnp.arange(NS, dtype=jnp.int32)
    cosine, sine = phase_pair(NS, index, index, 1.0 / math.sqrt(NS))
    cosine = cosine.astype(jnp.bfloat16)
    sine = sine.astype(jnp.bfloat16)
    return cosine, sine


def live_channels(flags, count):
    k = jnp.arange(flags.shape[0], dtype=jnp.int32)
    seen = jnp.sum(jnp.where(k[None, :] <= k[:, None], flags[None, :], 0), axis=1)
    j = jnp.arange(count, dtype=jnp.int32)
    return jnp.sum((seen[None, :] <= j[:, None]).astype(jnp.int32), axis=1)


def pfb_filter(voltages, n_frames, window):
    inputs = voltages.shape[0]
    frames = voltages.reshape(inputs, n_frames, 2 * CHANNELS).astype(jnp.float32)
    padded = jnp.pad(frames, ((0, 0), (TAPS - 1, TAPS - 1), (0, 0)))
    total = n_frames + TAPS - 1
    summed = 0.0
    for tap in range(TAPS):
        summed = summed + window[tap] * padded[:, tap : tap + total]
    return summed.astype(jnp.bfloat16)


def local_plain(voltages, feed_slot, channel_flags):
    n_frames = voltages.shape[1] // (2 * CHANNELS)
    n_time = lax.axis_size("tm")
    n_feed = lax.axis_size("feed")
    inputs = voltages.shape[0]
    live_count = LIVE_DEV * n_feed * n_time
    chans = LIVE_DEV * n_time
    live = live_channels(channel_flags, live_count)
    cosine, sine = phase_pair(
        2 * CHANNELS, live, jnp.arange(2 * CHANNELS, dtype=jnp.int32), 1.0 / math.sqrt(2 * CHANNELS)
    )
    coeffs = jnp.stack([cosine, -sine]).astype(jnp.bfloat16)
    filtered = pfb_filter(voltages, n_frames, pfb_window())
    spectra = jnp.einsum("rcs,ifs->rcfi", coeffs, filtered, preferred_element_type=jnp.float32)
    earlier = passed_along(spectra[:, :, n_frames:].astype(jnp.bfloat16), "tm", 1)
    spectra = spectra[:, :, :n_frames]
    spectra = jnp.concatenate(
        [spectra[:, :, : TAPS - 1] + earlier.astype(jnp.float32), spectra[:, :, TAPS - 1 :]], axis=2
    ).astype(jnp.bfloat16)
    turned = lax.all_to_all(
        spectra.reshape(2, n_feed, chans, n_frames, inputs), "feed", split_axis=1, concat_axis=1, tiled=True
    )
    slots = feed_slot.reshape(n_feed, inputs)
    onehot = (slots[:, :, None] == jnp.arange(n_feed * inputs, dtype=jnp.int32)).astype(jnp.bfloat16)
    cells = jnp.einsum(
        "rscfi,sin->rcfn", turned, onehot, preferred_element_type=jnp.float32
    ).astype(jnp.bfloat16)
    cells = cells.reshape(2, chans, n_frames, 2 * CYL, NS)
    cosine, sine = grid_table()
    table = jnp.stack([jnp.stack([cosine, -sine], axis=1), jnp.stack([sine, cosine], axis=1)])
    ns_out = jnp.einsum("rcfgm,rmqn->qcfgn", cells, table, preferred_element_type=jnp.float32)
    z = ns_out.reshape(2, chans, n_frames, 2, CYL, NS)
    re, im = z[0], z[1]
    r = [re[:, :, :, y] for y in range(CYL)]
    i = [im[:, :, :, y] for y in range(CYL)]
    t0r, t1r, t2r, t3r = r[0] + r[2], r[0] - r[2], r[1] + r[3], r[1] - r[3]
    t0i, t1i, t2i, t3i = i[0] + i[2], i[0] - i[2], i[1] + i[3], i[1] - i[3]
    beam_re = jnp.stack([t0r + t2r, t1r + t3i, t0r - t2r, t1r - t3i], axis=3)
    beam_im = jnp.stack([t0i + t2i, t1i - t3r, t0i - t2i, t1i + t3r], axis=3)
    beams = (jnp.stack([beam_re, beam_im]) * 0.5).astype(jnp.bfloat16)
    blocks = n_frames // UPCH
    beams = beams.reshape(2, chans, blocks, UPCH, 2, CYL * NS)
    index = jnp.arange(UPCH, dtype=jnp.int32)
    up_cos, up_sin = phase_pair(UPCH, index, index, 1.0 / math.sqrt(UPCH))
    up_cos = up_cos.astype(jnp.bfloat16)
    up_sin = up_sin.astype(jnp.bfloat16)
    up_table = jnp.stack([jnp.stack([up_cos, -up_sin], axis=1), jnp.stack([up_sin, up_cos], axis=1)])
    up = jnp.einsum("qcbupn,quvk->vcbkpn", beams, up_table, preferred_element_type=jnp.float32)
    power = jnp.sum(up * up, axis=(0, 2, 4)) * (1.0 / (2.0 * n_time * blocks))
    parts = lax.all_to_all(
        power.astype(jnp.bfloat16).reshape(n_time, LIVE_DEV, UPCH, CYL * NS), "tm", split_axis=0, concat_axis=0, tiled=True
    )
    return jnp.sum(parts.astype(jnp.float32), axis=0)


MESH = pl.DeviceIdType.MESH
NT = (((1,), (1,)), ((), ()))


def fused_kernel(
    n_feed, n_time, n_frames, scale,
    volt, trig, window, slots, t1, t2, upm, out,
    vp, coeffs, filt, tmp, send, recv, hist_out, hist_in, onehot, acc, beams, power, psend, precv,
    load_sem, own_sem, hist_sem, send_sem, recv_sem, psend_sem, precv_sem,
):
    me = lax.axis_index("feed")
    tm = lax.axis_index("tm")
    frame = 2 * CHANNELS
    past = TAPS - 1
    quads = n_frames // 4
    inputs = volt.shape[0]
    rows = coeffs.shape[0]
    own_rows = LIVE_DEV * UPCH

    def partner(m):
        far = lax.rem(me // 4 + m // 4, 2)
        near = lax.rem(lax.rem(me // 2, 2) + lax.rem(m // 2, 2), 2)
        return far * 4 + near * 2 + lax.rem(lax.rem(me, 2) + lax.rem(m, 2), 2)

    def load(f):
        return pltpu.make_async_copy(
            volt.at[:, f * frame : (f + 1) * frame], vp.at[f + past], load_sem.at[f]
        )

    order = list(range(1, n_frames)) + [0]
    for f in order:
        load(f).start()
    barrier = pltpu.get_barrier_semaphore()
    for o in range(1, n_feed):
        pl.semaphore_signal(barrier, inc=1, device_id={"feed": lax.rem(me + o, n_feed)}, device_id_type=MESH)
    for o in range(1, n_time):
        pl.semaphore_signal(barrier, inc=1, device_id={"tm": lax.rem(tm + o, n_time)}, device_id_type=MESH)
    pl.semaphore_wait(barrier, n_feed - 1 + n_time - 1)

    for k in range(frame // 128):
        value = trig[:, 256 + k : 257 + k] * trig[:, :128]
        value = value - trig[:, 256 + frame // 128 + k : 257 + frame // 128 + k] * trig[:, 128:256]
        coeffs[:, k * 128 : (k + 1) * 128] = (value * (1.0 / math.sqrt(frame))).astype(jnp.bfloat16)

    for t in range(past):
        vp[t] = jnp.zeros_like(vp[t])
        vp[n_frames + past + t] = jnp.zeros_like(vp[t])

    def spectra(f):
        width = 256

        def chunk(c, _):
            lanes = pl.ds(pl.multiple_of(c * width, width), width)
            total = window[0:1, lanes] * vp[f, :, lanes].astype(jnp.float32)
            for t in range(1, TAPS):
                total = total + window[t : t + 1, lanes] * vp[f + t, :, lanes].astype(jnp.float32)
            filt[:, lanes] = total.astype(jnp.bfloat16)
            return 0

        lax.fori_loop(0, frame // width, chunk, 0)
        return lax.dot_general(coeffs[...], filt[...], NT, preferred_element_type=jnp.float32)

    def hist_copy(to):
        return pltpu.make_async_remote_copy(
            src_ref=hist_out, dst_ref=hist_in, send_sem=hist_sem.at[0], recv_sem=hist_sem.at[1],
            device_id={"tm": to}, device_id_type=MESH,
        )

    def send_copy(q, m):
        to = partner(m)
        return pltpu.make_async_remote_copy(
            src_ref=send.at[q, to], dst_ref=recv.at[me, q],
            send_sem=send_sem.at[q, m], recv_sem=recv_sem.at[q, m],
            device_id={"feed": to}, device_id_type=MESH,
        )

    def arrival(q, m):
        back = partner(m)
        return pltpu.make_async_remote_copy(
            src_ref=send.at[q, back], dst_ref=recv.at[back, q],
            send_sem=send_sem.at[q, m], recv_sem=recv_sem.at[q, m],
            device_id={"feed": back}, device_id_type=MESH,
        )

    def own_copy(q):
        return pltpu.make_async_copy(send.at[q, me], recv.at[me, q], own_sem.at[q])

    def far_first(k):
        return lax.rem(k + n_feed // 2 - 1, n_feed - 1) + 1

    lower = lax.broadcasted_iota(jnp.int32, (8, inputs), 0) < 4

    def quad(q, first):
        def one(k, _):
            value = spectra(q * 4 + k)
            if first:
                value = value + jnp.where(k < past, 1.0, 0.0) * hist_in[jnp.minimum(k, past - 1)].astype(jnp.float32)
            tmp[k] = value
            return 0

        lax.fori_loop(0, 4, one, 0)

        def pack(d, _):
            parts = [[], []]
            at = pl.multiple_of(d * 24, 8)
            for pair in range(2):
                a0, b0, c0 = (tmp[2 * pair, pl.ds(at + 8 * k, 8)] for k in range(3))
                a1, b1, c1 = (tmp[2 * pair + 1, pl.ds(at + 8 * k, 8)] for k in range(3))
                parts[0] += [a0, a1, jnp.where(lower, b0, pltpu.roll(b1, 4, 0))]
                parts[1] += [c0, c1, jnp.where(lower, pltpu.roll(b0, 4, 0), b1)]
            send[q, d, 0] = jnp.concatenate(parts[0], axis=0).astype(jnp.bfloat16)
            send[q, d, 1] = jnp.concatenate(parts[1], axis=0).astype(jnp.bfloat16)
            return 0

        lax.fori_loop(0, n_feed, pack, 0)

        def start(k, _):
            send_copy(q, far_first(k)).start()
            return 0

        lax.fori_loop(0, n_feed - 1, start, 0)
        own_copy(q).start()

    def tail_frames():
        def tail_frame(k, _):
            hist_out[k] = spectra(n_frames + k).astype(jnp.bfloat16)
            return 0

        lax.fori_loop(0, past, tail_frame, 0)

        @pl.when(tm < n_time - 1)
        def _():
            hist_copy(lax.rem(tm + 1, n_time)).start()

    for f in range(1, 8):
        load(f).wait()
    quad(1, False)
    for q in range(2, quads):
        for f in range(4 * q, 4 * q + 4):
            load(f).wait()
        if q == quads - 1:
            tail_frames()
        quad(q, False)
    load(0).wait()

    @pl.when(tm > 0)
    def _():
        hist_copy(lax.rem(tm + n_time - 1, n_time)).wait_recv()

    @pl.when(tm == 0)
    def _():
        hist_in[...] = jnp.zeros_like(hist_in)

    quad(0, True)

    total = n_feed * inputs
    which = lax.broadcasted_iota(jnp.int32, (total, inputs), 0)

    def ones(s, _):
        onehot[s] = jnp.where(which == slots[s], 1.0, 0.0).astype(jnp.bfloat16)
        return 0

    lax.fori_loop(0, n_feed, ones, 0)

    step = 512

    def place(s, lo, hi, fresh):
        count = hi - lo
        block = recv[s, lo:hi].reshape(count * 96, inputs)

        def part(n, _):
            at = pl.multiple_of(n * step, step)
            got = lax.dot_general(block, onehot[s, pl.ds(at, step), :], NT, preferred_element_type=jnp.float32)
            got = got.reshape(count, 2, 48, step)
            if fresh:
                acc[lo:hi, :, :, pl.ds(at, step)] = got
            else:
                acc[lo:hi, :, :, pl.ds(at, step)] += got
            return 0

        lax.fori_loop(0, total // step, part, 0)

    def gather(lo, hi):
        for q in range(lo, hi):
            own_copy(q).wait()
        place(me, lo, hi, True)

        def source(k, _):
            for q in range(lo, hi):
                arrival(q, k + 1).wait_recv()
            place(partner(k + 1), lo, hi, False)
            return 0

        lax.fori_loop(0, n_feed - 1, source, 0)

    def beamform(lo, hi):
        count = hi - lo

        def cells(part, at):
            return acc[lo:hi, part, :, at : at + NS].reshape(count * 48, NS).astype(jnp.bfloat16)

        for p in range(2):
            z = []
            for y in range(CYL):
                at = (p * CYL + y) * NS
                value = jnp.dot(cells(0, at), t1[...], preferred_element_type=jnp.float32)
                value = value + jnp.dot(cells(1, at), t2[...], preferred_element_type=jnp.float32)
                z.append((value[:, :NS], value[:, NS:]))
            (r0, i0), (r1, i1), (r2, i2), (r3, i3) = z
            t0r, t1r, t2r, t3r = r0 + r2, r0 - r2, r1 + r3, r1 - r3
            t0i, t1i, t2i, t3i = i0 + i2, i0 - i2, i1 + i3, i1 - i3
            re = [t0r + t2r, t1r + t3i, t0r - t2r, t1r - t3i]
            im = [t0i + t2i, t1i - t3r, t0i - t2i, t1i + t3r]
            for e in range(CYL):
                at = (p * CYL + e) * NS
                for part, value in ((0, re[e]), (1, im[e])):
                    beams[part, lo:hi, :, at : at + NS] = (value * 0.5).astype(jnp.bfloat16).reshape(count, 48, NS)

    gather(1, quads)
    beamform(1, quads)
    gather(0, 1)
    beamform(0, 1)

    outs = upm.shape[0] // 2
    for e in range(CYL):
        summed = 0.0
        for p in range(2):
            at = (p * CYL + e) * NS
            up = jnp.dot(upm[...], beams[:, :, :, at : at + NS].reshape(-1, NS), preferred_element_type=jnp.float32)
            summed = summed + up[:outs] * up[:outs] + up[outs:] * up[outs:]
        summed = summed * scale
        for t in range(n_time):
            block = summed[t * own_rows : (t + 1) * own_rows]
            power[t, :, e * NS : (e + 1) * NS] = block
            psend[t, :, e * NS : (e + 1) * NS] = block.astype(jnp.bfloat16)

    def power_copy(o):
        to = lax.rem(tm + o, n_time)
        return pltpu.make_async_remote_copy(
            src_ref=psend.at[to], dst_ref=precv.at[o - 1],
            send_sem=psend_sem.at[o - 1], recv_sem=precv_sem.at[o - 1],
            device_id={"tm": to}, device_id_type=MESH,
        )

    for o in range(1, n_time):
        power_copy(o).start()
    result = power[tm]
    for o in range(1, n_time):
        power_copy(o).wait_recv()
        result = result + precv[o - 1].astype(jnp.float32)
    out[...] = result
    for o in range(1, n_time):
        power_copy(o).wait_send()

    def drain(k, _):
        for q in range(quads):
            send_copy(q, k + 1).wait_send()
        return 0

    lax.fori_loop(0, n_feed - 1, drain, 0)

    @pl.when(tm < n_time - 1)
    def _():
        hist_copy(lax.rem(tm + 1, n_time)).wait_send()


def row_order(quads):
    frames, chans = [], []
    for q in range(quads):
        for pair in range(2):
            f = 4 * q + 2 * pair
            frames += [f] * 8 + [f + 1] * 8 + [f] * 4 + [f + 1] * 4
            chans += list(range(8)) * 2 + list(range(8, 12)) * 2
    return np.array(frames), np.array(chans)


def rounded_pair(modulus, first, second):
    angle = (first[:, None] * second[None, :] % modulus) * (2.0 * np.pi / modulus)
    scale = 1.0 / np.sqrt(modulus)
    bf16 = jnp.bfloat16
    return (
        (np.cos(angle) * scale).astype(np.float32).astype(bf16),
        (np.sin(angle) * scale).astype(np.float32).astype(bf16),
    )


def window_table():
    length = TAPS * 2 * CHANNELS
    sample = np.arange(length)
    offset = (sample - length / 2 + 0.5) / (2 * CHANNELS)
    taper = 0.5 - 0.5 * np.cos(2.0 * np.pi * (sample + 0.5) / length)
    return (np.sinc(offset) * taper).astype(np.float32).reshape(TAPS, 2 * CHANNELS)


def local_fused(voltages, feed_slot, channel_flags):
    bf16 = jnp.bfloat16
    frame = 2 * CHANNELS
    inputs = voltages.shape[0]
    n_frames = voltages.shape[1] // frame
    n_time = lax.axis_size("tm")
    n_feed = lax.axis_size("feed")
    chans = LIVE_DEV * n_time
    quads = n_frames // 4
    live = live_channels(channel_flags, chans * n_feed).reshape(n_feed, chans)
    row_chan = jnp.concatenate([live, live[:, 8:], live[:, :8]], axis=1).reshape(-1)
    quarter = frame // 4
    shift = np.tile(np.where(np.arange(2 * chans) >= chans, quarter, 0), n_feed)
    fine = np.arange(128)
    coarse = np.arange(frame // 128) * 128
    step = jnp.array(np.concatenate([fine, fine, coarse, coarse]), jnp.int32)
    lag = np.concatenate([fine * 0, fine * 0 + quarter, coarse * 0, coarse * 0 + quarter])
    turned = np.concatenate([fine * 0, fine * 0, coarse * 0 + 1, coarse * 0 + 1])
    extra = jnp.array(shift[:, None] * turned[None, :] + frame - lag[None, :], jnp.int32)
    product = (row_chan[:, None] * step[None, :] + extra) % frame
    trig = jnp.cos(product.astype(jnp.float32) * (2.0 * jnp.pi / frame))
    index = np.arange(NS)
    c, d = rounded_pair(NS, index, index)
    t1 = jnp.array(np.concatenate([c, -d], axis=1))
    t2 = jnp.array(np.concatenate([d, c], axis=1))
    frames, row_ch = row_order(quads)
    up_cos, up_sin = rounded_pair(UPCH, np.arange(UPCH), frames)
    same = (np.arange(chans)[:, None] == row_ch[None, :])[:, None, :].astype(np.float32)
    cm = (same * up_cos.astype(np.float32)[None]).reshape(chans * UPCH, -1)
    sm = (same * up_sin.astype(np.float32)[None]).reshape(chans * UPCH, -1)
    upm = np.concatenate([np.concatenate([cm, sm], 1), np.concatenate([-sm, cm], 1)], 0)
    upm = jnp.array(upm.astype(bf16))
    rows = 2 * chans * n_feed
    total = n_feed * inputs
    own_rows = LIVE_DEV * UPCH
    vmem = pl.BlockSpec(memory_space=pltpu.VMEM)
    dma = pltpu.SemaphoreType.DMA
    result = pl.pallas_call(
        functools.partial(fused_kernel, n_feed, n_time, n_frames, 1.0 / (2.0 * n_time)),
        out_shape=jax.ShapeDtypeStruct((own_rows, CYL * NS), jnp.float32),
        in_specs=[pl.BlockSpec(memory_space=pl.ANY)] + [vmem] * 6,
        out_specs=vmem,
        scratch_shapes=[
            pltpu.VMEM((n_frames + 2 * TAPS - 2, inputs, frame), bf16),
            pltpu.VMEM((rows, frame), bf16),
            pltpu.VMEM((inputs, frame), bf16),
            pltpu.VMEM((4, rows, inputs), jnp.float32),
            pltpu.VMEM((quads, n_feed, 2, 48, inputs), bf16),
            pltpu.VMEM((n_feed, quads, 2, 48, inputs), bf16),
            pltpu.VMEM((TAPS - 1, rows, inputs), bf16),
            pltpu.VMEM((TAPS - 1, rows, inputs), bf16),
            pltpu.VMEM((n_feed, total, inputs), bf16),
            pltpu.VMEM((quads, 2, 48, total), jnp.float32),
            pltpu.VMEM((2, quads, 48, total), bf16),
            pltpu.VMEM((n_time, own_rows, CYL * NS), jnp.float32),
            pltpu.VMEM((n_time, own_rows, CYL * NS), bf16),
            pltpu.VMEM((n_time - 1, own_rows, CYL * NS), bf16),
            dma((n_frames,)),
            dma((quads,)),
            dma((2,)),
            dma((quads, n_feed)),
            dma((quads, n_feed)),
            dma((n_time - 1,)),
            dma((n_time - 1,)),
        ],
        compiler_params=pltpu.CompilerParams(
            collective_id=0, has_side_effects=True, vmem_limit_bytes=62 * 1024 * 1024
        ),
    )(voltages, trig, jnp.array(window_table()), feed_slot.reshape(n_feed, 1, inputs), t1, t2, upm)
    return result.reshape(LIVE_DEV, UPCH, CYL * NS)


def local(voltages, feed_slot, channel_flags):
    fits = (
        voltages.shape[0] == NS
        and voltages.shape[1] == UPCH * 2 * CHANNELS
        and lax.axis_size("tm") == 4
        and lax.axis_size("feed") == 8
        and lax.axis_size("feed") * voltages.shape[0] == 2 * CYL * NS
    )
    return (local_fused if fits else local_plain)(voltages, feed_slot, channel_flags)


def solution(mesh):
    in_specs = (P("feed", "tm"), P(), P())
    out_specs = P(("feed", "tm"), None, None)
    return jax.shard_map(local, mesh=mesh, in_specs=in_specs, out_specs=out_specs, check_vma=False)
```

```python
import math

import functools

import jax
import jax.numpy as jnp
import numpy as np
from jax import lax
from jax.experimental import pallas as pl
from jax.experimental.pallas import tpu as pltpu
from jax.sharding import PartitionSpec as P

CHANNELS = 1024
TAPS = 4
CYL = 4
NS = 256
UPCH = 16
LIVE_DEV = 3


def passed_along(block, axis, distance):
    devices = range(lax.axis_size(axis))
    route = [(i - distance, i) for i in devices if i - distance in devices]
    return lax.ppermute(block, axis, route)


def pfb_window():
    length = TAPS * 2 * CHANNELS
    sample = jnp.arange(length, dtype=jnp.float32)
    offset = (sample - length / 2 + 0.5) / (2 * CHANNELS)
    taper = 0.5 - 0.5 * jnp.cos(2.0 * jnp.pi * (sample + 0.5) / length)
    return (jnp.sinc(offset) * taper).reshape(TAPS, 2 * CHANNELS)


def phase_pair(modulus, first, second, scale):
    product = first[:, None] * second[None, :] % modulus
    angle = product.astype(jnp.float32) * (2.0 * jnp.pi / modulus)
    return (jnp.cos(angle) * scale, jnp.sin(angle) * scale)


def grid_table():
    index = jnp.arange(NS, dtype=jnp.int32)
    cosine, sine = phase_pair(NS, index, index, 1.0 / math.sqrt(NS))
    cosine = cosine.astype(jnp.bfloat16)
    sine = sine.astype(jnp.bfloat16)
    return cosine, sine


def live_channels(flags, count):
    k = jnp.arange(flags.shape[0], dtype=jnp.int32)
    seen = jnp.sum(jnp.where(k[None, :] <= k[:, None], flags[None, :], 0), axis=1)
    j = jnp.arange(count, dtype=jnp.int32)
    return jnp.sum((seen[None, :] <= j[:, None]).astype(jnp.int32), axis=1)


def pfb_filter(voltages, n_frames, window):
    inputs = voltages.shape[0]
    frames = voltages.reshape(inputs, n_frames, 2 * CHANNELS).astype(jnp.float32)
    padded = jnp.pad(frames, ((0, 0), (TAPS - 1, TAPS - 1), (0, 0)))
    total = n_frames + TAPS - 1
    summed = 0.0
    for tap in range(TAPS):
        summed = summed + window[tap] * padded[:, tap : tap + total]
    return summed.astype(jnp.bfloat16)


def local_plain(voltages, feed_slot, channel_flags):
    n_frames = voltages.shape[1] // (2 * CHANNELS)
    n_time = lax.axis_size("tm")
    n_feed = lax.axis_size("feed")
    inputs = voltages.shape[0]
    live_count = LIVE_DEV * n_feed * n_time
    chans = LIVE_DEV * n_time
    live = live_channels(channel_flags, live_count)
    cosine, sine = phase_pair(
        2 * CHANNELS, live, jnp.arange(2 * CHANNELS, dtype=jnp.int32), 1.0 / math.sqrt(2 * CHANNELS)
    )
    coeffs = jnp.stack([cosine, -sine]).astype(jnp.bfloat16)
    filtered = pfb_filter(voltages, n_frames, pfb_window())
    spectra = jnp.einsum("rcs,ifs->rcfi", coeffs, filtered, preferred_element_type=jnp.float32)
    earlier = passed_along(spectra[:, :, n_frames:].astype(jnp.bfloat16), "tm", 1)
    spectra = spectra[:, :, :n_frames]
    spectra = jnp.concatenate(
        [spectra[:, :, : TAPS - 1] + earlier.astype(jnp.float32), spectra[:, :, TAPS - 1 :]], axis=2
    ).astype(jnp.bfloat16)
    turned = lax.all_to_all(
        spectra.reshape(2, n_feed, chans, n_frames, inputs), "feed", split_axis=1, concat_axis=1, tiled=True
    )
    slots = feed_slot.reshape(n_feed, inputs)
    onehot = (slots[:, :, None] == jnp.arange(n_feed * inputs, dtype=jnp.int32)).astype(jnp.bfloat16)
    cells = jnp.einsum(
        "rscfi,sin->rcfn", turned, onehot, preferred_element_type=jnp.float32
    ).astype(jnp.bfloat16)
    cells = cells.reshape(2, chans, n_frames, 2 * CYL, NS)
    cosine, sine = grid_table()
    table = jnp.stack([jnp.stack([cosine, -sine], axis=1), jnp.stack([sine, cosine], axis=1)])
    ns_out = jnp.einsum("rcfgm,rmqn->qcfgn", cells, table, preferred_element_type=jnp.float32)
    z = ns_out.reshape(2, chans, n_frames, 2, CYL, NS)
    re, im = z[0], z[1]
    r = [re[:, :, :, y] for y in range(CYL)]
    i = [im[:, :, :, y] for y in range(CYL)]
    t0r, t1r, t2r, t3r = r[0] + r[2], r[0] - r[2], r[1] + r[3], r[1] - r[3]
    t0i, t1i, t2i, t3i = i[0] + i[2], i[0] - i[2], i[1] + i[3], i[1] - i[3]
    beam_re = jnp.stack([t0r + t2r, t1r + t3i, t0r - t2r, t1r - t3i], axis=3)
    beam_im = jnp.stack([t0i + t2i, t1i - t3r, t0i - t2i, t1i + t3r], axis=3)
    beams = (jnp.stack([beam_re, beam_im]) * 0.5).astype(jnp.bfloat16)
    blocks = n_frames // UPCH
    beams = beams.reshape(2, chans, blocks, UPCH, 2, CYL * NS)
    index = jnp.arange(UPCH, dtype=jnp.int32)
    up_cos, up_sin = phase_pair(UPCH, index, index, 1.0 / math.sqrt(UPCH))
    up_cos = up_cos.astype(jnp.bfloat16)
    up_sin = up_sin.astype(jnp.bfloat16)
    up_table = jnp.stack([jnp.stack([up_cos, -up_sin], axis=1), jnp.stack([up_sin, up_cos], axis=1)])
    up = jnp.einsum("qcbupn,quvk->vcbkpn", beams, up_table, preferred_element_type=jnp.float32)
    power = jnp.sum(up * up, axis=(0, 2, 4)) * (1.0 / (2.0 * n_time * blocks))
    parts = lax.all_to_all(
        power.astype(jnp.bfloat16).reshape(n_time, LIVE_DEV, UPCH, CYL * NS), "tm", split_axis=0, concat_axis=0, tiled=True
    )
    return jnp.sum(parts.astype(jnp.float32), axis=0)


MESH = pl.DeviceIdType.MESH
NT = (((1,), (1,)), ((), ()))


def fused_kernel(
    n_feed, n_time, n_frames, scale,
    volt, trig, window, slots, t1, t2, upm, out,
    vp, coeffs, filt, tmp, send, recv, hist_out, hist_in, onehot, acc, beams, power, psend, precv,
    load_sem, own_sem, hist_sem, send_sem, recv_sem, psend_sem, precv_sem,
):
    me = lax.axis_index("feed")
    tm = lax.axis_index("tm")
    frame = 2 * CHANNELS
    past = TAPS - 1
    quads = n_frames // 4
    inputs = volt.shape[0]
    rows = coeffs.shape[0]
    own_rows = LIVE_DEV * UPCH

    def partner(m):
        far = lax.rem(me // 4 + m // 4, 2)
        near = lax.rem(lax.rem(me // 2, 2) + lax.rem(m // 2, 2), 2)
        return far * 4 + near * 2 + lax.rem(lax.rem(me, 2) + lax.rem(m, 2), 2)

    def load(f):
        return pltpu.make_async_copy(
            volt.at[:, f * frame : (f + 1) * frame], vp.at[f + past], load_sem.at[f]
        )

    order = list(range(1, n_frames)) + [0]
    for f in order:
        load(f).start()
    barrier = pltpu.get_barrier_semaphore()
    for o in range(1, n_feed):
        pl.semaphore_signal(barrier, inc=1, device_id={"feed": lax.rem(me + o, n_feed)}, device_id_type=MESH)
    for o in range(1, n_time):
        pl.semaphore_signal(barrier, inc=1, device_id={"tm": lax.rem(tm + o, n_time)}, device_id_type=MESH)
    pl.semaphore_wait(barrier, n_feed - 1 + n_time - 1)

    for k in range(frame // 128):
        value = trig[:, 256 + k : 257 + k] * trig[:, :128]
        value = value - trig[:, 256 + frame // 128 + k : 257 + frame // 128 + k] * trig[:, 128:256]
        coeffs[:, k * 128 : (k + 1) * 128] = (value * (1.0 / math.sqrt(frame))).astype(jnp.bfloat16)

    for t in range(past):
        vp[t] = jnp.zeros_like(vp[t])
        vp[n_frames + past + t] = jnp.zeros_like(vp[t])

    def spectra(f):
        width = 256

        def chunk(c, _):
            lanes = pl.ds(pl.multiple_of(c * width, width), width)
            total = window[0:1, lanes] * vp[f, :, lanes].astype(jnp.float32)
            for t in range(1, TAPS):
                total = total + window[t : t + 1, lanes] * vp[f + t, :, lanes].astype(jnp.float32)
            filt[:, lanes] = total.astype(jnp.bfloat16)
            return 0

        lax.fori_loop(0, frame // width, chunk, 0)
        return lax.dot_general(coeffs[...], filt[...], NT, preferred_element_type=jnp.float32)

    def hist_copy(to):
        return pltpu.make_async_remote_copy(
            src_ref=hist_out, dst_ref=hist_in, send_sem=hist_sem.at[0], recv_sem=hist_sem.at[1],
            device_id={"tm": to}, device_id_type=MESH,
        )

    def send_copy(q, m):
        to = partner(m)
        return pltpu.make_async_remote_copy(
            src_ref=send.at[q, to], dst_ref=recv.at[me, q],
            send_sem=send_sem.at[q, m], recv_sem=recv_sem.at[q, m],
            device_id={"feed": to}, device_id_type=MESH,
        )

    def arrival(q, m):
        back = partner(m)
        return pltpu.make_async_remote_copy(
            src_ref=send.at[q, back], dst_ref=recv.at[back, q],
            send_sem=send_sem.at[q, m], recv_sem=recv_sem.at[q, m],
            device_id={"feed": back}, device_id_type=MESH,
        )

    def own_copy(q):
        return pltpu.make_async_copy(send.at[q, me], recv.at[me, q], own_sem.at[q])

    def far_first(k):
        return lax.rem(k + n_feed // 2 - 1, n_feed - 1) + 1

    lower = lax.broadcasted_iota(jnp.int32, (8, inputs), 0) < 4

    def quad(q, first):
        def one(k, _):
            value = spectra(q * 4 + k)
            if first:
                value = value + jnp.where(k < past, 1.0, 0.0) * hist_in[jnp.minimum(k, past - 1)].astype(jnp.float32)
            tmp[k] = value
            return 0

        lax.fori_loop(0, 4, one, 0)

        def pack(d, _):
            parts = [[], []]
            at = pl.multiple_of(d * 24, 8)
            for pair in range(2):
                a0, b0, c0 = (tmp[2 * pair, pl.ds(at + 8 * k, 8)] for k in range(3))
                a1, b1, c1 = (tmp[2 * pair + 1, pl.ds(at + 8 * k, 8)] for k in range(3))
                parts[0] += [a0, a1, jnp.where(lower, b0, pltpu.roll(b1, 4, 0))]
                parts[1] += [c0, c1, jnp.where(lower, pltpu.roll(b0, 4, 0), b1)]
            send[q, d, 0] = jnp.concatenate(parts[0], axis=0).astype(jnp.bfloat16)
            send[q, d, 1] = jnp.concatenate(parts[1], axis=0).astype(jnp.bfloat16)
            return 0

        lax.fori_loop(0, n_feed, pack, 0)

        def start(k, _):
            send_copy(q, far_first(k)).start()
            return 0

        lax.fori_loop(0, n_feed - 1, start, 0)
        own_copy(q).start()

    def tail_frames():
        def tail_frame(k, _):
            hist_out[k] = spectra(n_frames + k).astype(jnp.bfloat16)
            return 0

        lax.fori_loop(0, past, tail_frame, 0)

        @pl.when(tm < n_time - 1)
        def _():
            hist_copy(lax.rem(tm + 1, n_time)).start()

    for f in range(1, 8):
        load(f).wait()
    quad(1, False)
    for q in range(2, quads):
        for f in range(4 * q, 4 * q + 4):
            load(f).wait()
        if q == quads - 1:
            tail_frames()
        quad(q, False)
    load(0).wait()

    @pl.when(tm > 0)
    def _():
        hist_copy(lax.rem(tm + n_time - 1, n_time)).wait_recv()

    @pl.when(tm == 0)
    def _():
        hist_in[...] = jnp.zeros_like(hist_in)

    quad(0, True)

    total = n_feed * inputs
    which = lax.broadcasted_iota(jnp.int32, (total, inputs), 0)

    def ones(s, _):
        onehot[s] = jnp.where(which == slots[s], 1.0, 0.0).astype(jnp.bfloat16)
        return 0

    lax.fori_loop(0, n_feed, ones, 0)

    step = 512

    def place(s, lo, hi, fresh):
        count = hi - lo
        block = recv[s, lo:hi].reshape(count * 96, inputs)

        def part(n, _):
            at = pl.multiple_of(n * step, step)
            got = lax.dot_general(block, onehot[s, pl.ds(at, step), :], NT, preferred_element_type=jnp.float32)
            got = got.reshape(count, 2, 48, step)
            if fresh:
                acc[lo:hi, :, :, pl.ds(at, step)] = got
            else:
                acc[lo:hi, :, :, pl.ds(at, step)] += got
            return 0

        lax.fori_loop(0, total // step, part, 0)

    def gather(lo, hi):
        for q in range(lo, hi):
            own_copy(q).wait()
        place(me, lo, hi, True)

        def source(k, _):
            for q in range(lo, hi):
                arrival(q, k + 1).wait_recv()
            place(partner(k + 1), lo, hi, False)
            return 0

        lax.fori_loop(0, n_feed - 1, source, 0)

    def beamform(lo, hi):
        count = hi - lo

        def cells(part, at):
            return acc[lo:hi, part, :, at : at + NS].reshape(count * 48, NS).astype(jnp.bfloat16)

        stacked = [jnp.concatenate([cells(part, g * NS) for g in range(2 * CYL)], axis=0) for part in range(2)]
        value = jnp.dot(stacked[0], t1[...], preferred_element_type=jnp.float32)
        value = value + jnp.dot(stacked[1], t2[...], preferred_element_type=jnp.float32)
        for p in range(2):
            z = []
            for y in range(CYL):
                one = value[(p * CYL + y) * count * 48 : (p * CYL + y + 1) * count * 48]
                z.append((one[:, :NS], one[:, NS:]))
            (r0, i0), (r1, i1), (r2, i2), (r3, i3) = z
            t0r, t1r, t2r, t3r = r0 + r2, r0 - r2, r1 + r3, r1 - r3
            t0i, t1i, t2i, t3i = i0 + i2, i0 - i2, i1 + i3, i1 - i3
            re = [t0r + t2r, t1r + t3i, t0r - t2r, t1r - t3i]
            im = [t0i + t2i, t1i - t3r, t0i - t2i, t1i + t3r]
            for e in range(CYL):
                at = (p * CYL + e) * NS
                for part, beam in ((0, re[e]), (1, im[e])):
                    beams[part, lo:hi, :, at : at + NS] = (beam * 0.5).astype(jnp.bfloat16).reshape(count, 48, NS)

    gather(1, quads)
    beamform(1, quads)
    gather(0, 1)
    beamform(0, 1)

    def power_copy(o, e):
        to = lax.rem(tm + o, n_time)
        return pltpu.make_async_remote_copy(
            src_ref=psend.at[e, to], dst_ref=precv.at[o - 1, e],
            send_sem=psend_sem.at[o - 1, e], recv_sem=precv_sem.at[o - 1, e],
            device_id={"tm": to}, device_id_type=MESH,
        )

    outs = upm.shape[0] // 2
    for e in range(CYL):
        summed = 0.0
        for p in range(2):
            at = (p * CYL + e) * NS
            up = jnp.dot(upm[...], beams[:, :, :, at : at + NS].reshape(-1, NS), preferred_element_type=jnp.float32)
            summed = summed + up[:outs] * up[:outs] + up[outs:] * up[outs:]
        summed = (summed * scale).reshape(n_time, own_rows, NS)
        power[e] = summed
        psend[e] = summed.astype(jnp.bfloat16)
        for o in range(1, n_time):
            power_copy(o, e).start()
    for e in range(CYL):
        result = power[e, tm]
        for o in range(1, n_time):
            power_copy(o, e).wait_recv()
            result = result + precv[o - 1, e].astype(jnp.float32)
        out[:, e * NS : (e + 1) * NS] = result
    for e in range(CYL):
        for o in range(1, n_time):
            power_copy(o, e).wait_send()

    def drain(k, _):
        for q in range(quads):
            send_copy(q, k + 1).wait_send()
        return 0

    lax.fori_loop(0, n_feed - 1, drain, 0)

    @pl.when(tm < n_time - 1)
    def _():
        hist_copy(lax.rem(tm + 1, n_time)).wait_send()


def row_order(quads):
    frames, chans = [], []
    for q in range(quads):
        for pair in range(2):
            f = 4 * q + 2 * pair
            frames += [f] * 8 + [f + 1] * 8 + [f] * 4 + [f + 1] * 4
            chans += list(range(8)) * 2 + list(range(8, 12)) * 2
    return np.array(frames), np.array(chans)


def rounded_pair(modulus, first, second):
    angle = (first[:, None] * second[None, :] % modulus) * (2.0 * np.pi / modulus)
    scale = 1.0 / np.sqrt(modulus)
    bf16 = jnp.bfloat16
    return (
        (np.cos(angle) * scale).astype(np.float32).astype(bf16),
        (np.sin(angle) * scale).astype(np.float32).astype(bf16),
    )


def window_table():
    length = TAPS * 2 * CHANNELS
    sample = np.arange(length)
    offset = (sample - length / 2 + 0.5) / (2 * CHANNELS)
    taper = 0.5 - 0.5 * np.cos(2.0 * np.pi * (sample + 0.5) / length)
    return (np.sinc(offset) * taper).astype(np.float32).reshape(TAPS, 2 * CHANNELS)


def local_fused(voltages, feed_slot, channel_flags):
    bf16 = jnp.bfloat16
    frame = 2 * CHANNELS
    inputs = voltages.shape[0]
    n_frames = voltages.shape[1] // frame
    n_time = lax.axis_size("tm")
    n_feed = lax.axis_size("feed")
    chans = LIVE_DEV * n_time
    quads = n_frames // 4
    live = live_channels(channel_flags, chans * n_feed).reshape(n_feed, chans)
    row_chan = jnp.concatenate([live, live[:, 8:], live[:, :8]], axis=1).reshape(-1)
    quarter = frame // 4
    shift = np.tile(np.where(np.arange(2 * chans) >= chans, quarter, 0), n_feed)
    fine = np.arange(128)
    coarse = np.arange(frame // 128) * 128
    step = jnp.array(np.concatenate([fine, fine, coarse, coarse]), jnp.int32)
    lag = np.concatenate([fine * 0, fine * 0 + quarter, coarse * 0, coarse * 0 + quarter])
    turned = np.concatenate([fine * 0, fine * 0, coarse * 0 + 1, coarse * 0 + 1])
    extra = jnp.array(shift[:, None] * turned[None, :] + frame - lag[None, :], jnp.int32)
    product = (row_chan[:, None] * step[None, :] + extra) & (frame - 1)
    trig = jnp.cos(product.astype(jnp.float32) * (2.0 * jnp.pi / frame))
    index = np.arange(NS)
    c, d = rounded_pair(NS, index, index)
    t1 = jnp.array(np.concatenate([c, -d], axis=1))
    t2 = jnp.array(np.concatenate([d, c], axis=1))
    frames, row_ch = row_order(quads)
    up_cos, up_sin = rounded_pair(UPCH, np.arange(UPCH), frames)
    same = (np.arange(chans)[:, None] == row_ch[None, :])[:, None, :].astype(np.float32)
    cm = (same * up_cos.astype(np.float32)[None]).reshape(chans * UPCH, -1)
    sm = (same * up_sin.astype(np.float32)[None]).reshape(chans * UPCH, -1)
    upm = np.concatenate([np.concatenate([cm, sm], 1), np.concatenate([-sm, cm], 1)], 0)
    upm = jnp.array(upm.astype(bf16))
    rows = 2 * chans * n_feed
    total = n_feed * inputs
    own_rows = LIVE_DEV * UPCH
    vmem = pl.BlockSpec(memory_space=pltpu.VMEM)
    dma = pltpu.SemaphoreType.DMA
    result = pl.pallas_call(
        functools.partial(fused_kernel, n_feed, n_time, n_frames, 1.0 / (2.0 * n_time)),
        out_shape=jax.ShapeDtypeStruct((own_rows, CYL * NS), jnp.float32),
        in_specs=[pl.BlockSpec(memory_space=pl.ANY)] + [vmem] * 6,
        out_specs=vmem,
        scratch_shapes=[
            pltpu.VMEM((n_frames + 2 * TAPS - 2, inputs, frame), bf16),
            pltpu.VMEM((rows, frame), bf16),
            pltpu.VMEM((inputs, frame), bf16),
            pltpu.VMEM((4, rows, inputs), jnp.float32),
            pltpu.VMEM((quads, n_feed, 2, 48, inputs), bf16),
            pltpu.VMEM((n_feed, quads, 2, 48, inputs), bf16),
            pltpu.VMEM((TAPS - 1, rows, inputs), bf16),
            pltpu.VMEM((TAPS - 1, rows, inputs), bf16),
            pltpu.VMEM((n_feed, total, inputs), bf16),
            pltpu.VMEM((quads, 2, 48, total), jnp.float32),
            pltpu.VMEM((2, quads, 48, total), bf16),
            pltpu.VMEM((CYL, n_time, own_rows, NS), jnp.float32),
            pltpu.VMEM((CYL, n_time, own_rows, NS), bf16),
            pltpu.VMEM((n_time - 1, CYL, own_rows, NS), bf16),
            dma((n_frames,)),
            dma((quads,)),
            dma((2,)),
            dma((quads, n_feed)),
            dma((quads, n_feed)),
            dma((n_time - 1, CYL)),
            dma((n_time - 1, CYL)),
        ],
        compiler_params=pltpu.CompilerParams(
            collective_id=0, has_side_effects=True, vmem_limit_bytes=62 * 1024 * 1024
        ),
    )(voltages, trig, jnp.array(window_table()), feed_slot.reshape(n_feed, 1, inputs), t1, t2, upm)
    return result.reshape(LIVE_DEV, UPCH, CYL * NS)


def local(voltages, feed_slot, channel_flags):
    fits = (
        voltages.shape[0] == NS
        and voltages.shape[1] == UPCH * 2 * CHANNELS
        and lax.axis_size("tm") == 4
        and lax.axis_size("feed") == 8
        and lax.axis_size("feed") * voltages.shape[0] == 2 * CYL * NS
    )
    return (local_fused if fits else local_plain)(voltages, feed_slot, channel_flags)


def solution(mesh):
    in_specs = (P("feed", "tm"), P(), P())
    out_specs = P(("feed", "tm"), None, None)
    return jax.shard_map(local, mesh=mesh, in_specs=in_specs, out_specs=out_specs, check_vma=False)
```

```python
import math

import functools

import jax
import jax.numpy as jnp
import numpy as np
from jax import lax
from jax.experimental import pallas as pl
from jax.experimental.pallas import tpu as pltpu
from jax.sharding import PartitionSpec as P

CHANNELS = 1024
TAPS = 4
CYL = 4
NS = 256
UPCH = 16
LIVE_DEV = 3


def passed_along(block, axis, distance):
    devices = range(lax.axis_size(axis))
    route = [(i - distance, i) for i in devices if i - distance in devices]
    return lax.ppermute(block, axis, route)


def pfb_window():
    length = TAPS * 2 * CHANNELS
    sample = jnp.arange(length, dtype=jnp.float32)
    offset = (sample - length / 2 + 0.5) / (2 * CHANNELS)
    taper = 0.5 - 0.5 * jnp.cos(2.0 * jnp.pi * (sample + 0.5) / length)
    return (jnp.sinc(offset) * taper).reshape(TAPS, 2 * CHANNELS)


def phase_pair(modulus, first, second, scale):
    product = first[:, None] * second[None, :] % modulus
    angle = product.astype(jnp.float32) * (2.0 * jnp.pi / modulus)
    return (jnp.cos(angle) * scale, jnp.sin(angle) * scale)


def grid_table():
    index = jnp.arange(NS, dtype=jnp.int32)
    cosine, sine = phase_pair(NS, index, index, 1.0 / math.sqrt(NS))
    cosine = cosine.astype(jnp.bfloat16)
    sine = sine.astype(jnp.bfloat16)
    return cosine, sine


def live_channels(flags, count):
    k = jnp.arange(flags.shape[0], dtype=jnp.int32)
    seen = jnp.sum(jnp.where(k[None, :] <= k[:, None], flags[None, :], 0), axis=1)
    j = jnp.arange(count, dtype=jnp.int32)
    return jnp.sum((seen[None, :] <= j[:, None]).astype(jnp.int32), axis=1)


def pfb_filter(voltages, n_frames, window):
    inputs = voltages.shape[0]
    frames = voltages.reshape(inputs, n_frames, 2 * CHANNELS).astype(jnp.float32)
    padded = jnp.pad(frames, ((0, 0), (TAPS - 1, TAPS - 1), (0, 0)))
    total = n_frames + TAPS - 1
    summed = 0.0
    for tap in range(TAPS):
        summed = summed + window[tap] * padded[:, tap : tap + total]
    return summed.astype(jnp.bfloat16)


def local_plain(voltages, feed_slot, channel_flags):
    n_frames = voltages.shape[1] // (2 * CHANNELS)
    n_time = lax.axis_size("tm")
    n_feed = lax.axis_size("feed")
    inputs = voltages.shape[0]
    live_count = LIVE_DEV * n_feed * n_time
    chans = LIVE_DEV * n_time
    live = live_channels(channel_flags, live_count)
    cosine, sine = phase_pair(
        2 * CHANNELS, live, jnp.arange(2 * CHANNELS, dtype=jnp.int32), 1.0 / math.sqrt(2 * CHANNELS)
    )
    coeffs = jnp.stack([cosine, -sine]).astype(jnp.bfloat16)
    filtered = pfb_filter(voltages, n_frames, pfb_window())
    spectra = jnp.einsum("rcs,ifs->rcfi", coeffs, filtered, preferred_element_type=jnp.float32)
    earlier = passed_along(spectra[:, :, n_frames:].astype(jnp.bfloat16), "tm", 1)
    spectra = spectra[:, :, :n_frames]
    spectra = jnp.concatenate(
        [spectra[:, :, : TAPS - 1] + earlier.astype(jnp.float32), spectra[:, :, TAPS - 1 :]], axis=2
    ).astype(jnp.bfloat16)
    turned = lax.all_to_all(
        spectra.reshape(2, n_feed, chans, n_frames, inputs), "feed", split_axis=1, concat_axis=1, tiled=True
    )
    slots = feed_slot.reshape(n_feed, inputs)
    onehot = (slots[:, :, None] == jnp.arange(n_feed * inputs, dtype=jnp.int32)).astype(jnp.bfloat16)
    cells = jnp.einsum(
        "rscfi,sin->rcfn", turned, onehot, preferred_element_type=jnp.float32
    ).astype(jnp.bfloat16)
    cells = cells.reshape(2, chans, n_frames, 2 * CYL, NS)
    cosine, sine = grid_table()
    table = jnp.stack([jnp.stack([cosine, -sine], axis=1), jnp.stack([sine, cosine], axis=1)])
    ns_out = jnp.einsum("rcfgm,rmqn->qcfgn", cells, table, preferred_element_type=jnp.float32)
    z = ns_out.reshape(2, chans, n_frames, 2, CYL, NS)
    re, im = z[0], z[1]
    r = [re[:, :, :, y] for y in range(CYL)]
    i = [im[:, :, :, y] for y in range(CYL)]
    t0r, t1r, t2r, t3r = r[0] + r[2], r[0] - r[2], r[1] + r[3], r[1] - r[3]
    t0i, t1i, t2i, t3i = i[0] + i[2], i[0] - i[2], i[1] + i[3], i[1] - i[3]
    beam_re = jnp.stack([t0r + t2r, t1r + t3i, t0r - t2r, t1r - t3i], axis=3)
    beam_im = jnp.stack([t0i + t2i, t1i - t3r, t0i - t2i, t1i + t3r], axis=3)
    beams = (jnp.stack([beam_re, beam_im]) * 0.5).astype(jnp.bfloat16)
    blocks = n_frames // UPCH
    beams = beams.reshape(2, chans, blocks, UPCH, 2, CYL * NS)
    index = jnp.arange(UPCH, dtype=jnp.int32)
    up_cos, up_sin = phase_pair(UPCH, index, index, 1.0 / math.sqrt(UPCH))
    up_cos = up_cos.astype(jnp.bfloat16)
    up_sin = up_sin.astype(jnp.bfloat16)
    up_table = jnp.stack([jnp.stack([up_cos, -up_sin], axis=1), jnp.stack([up_sin, up_cos], axis=1)])
    up = jnp.einsum("qcbupn,quvk->vcbkpn", beams, up_table, preferred_element_type=jnp.float32)
    power = jnp.sum(up * up, axis=(0, 2, 4)) * (1.0 / (2.0 * n_time * blocks))
    parts = lax.all_to_all(
        power.astype(jnp.bfloat16).reshape(n_time, LIVE_DEV, UPCH, CYL * NS), "tm", split_axis=0, concat_axis=0, tiled=True
    )
    return jnp.sum(parts.astype(jnp.float32), axis=0)


MESH = pl.DeviceIdType.MESH
NT = (((1,), (1,)), ((), ()))


def fused_kernel(
    n_feed, n_time, n_frames, scale,
    volt, trig, window, slots, t1, t2, upm, out,
    vp, coeffs, filt, tmp, send, recv, hist_out, hist_in, onehot, acc, beams, power, psend, precv,
    load_sem, own_sem, hist_sem, send_sem, recv_sem, psend_sem, precv_sem,
):
    me = lax.axis_index("feed")
    tm = lax.axis_index("tm")
    frame = 2 * CHANNELS
    past = TAPS - 1
    quads = n_frames // 4
    inputs = volt.shape[0]
    rows = coeffs.shape[0]
    own_rows = LIVE_DEV * UPCH

    def partner(m):
        far = lax.rem(me // 4 + m // 4, 2)
        near = lax.rem(lax.rem(me // 2, 2) + lax.rem(m // 2, 2), 2)
        return far * 4 + near * 2 + lax.rem(lax.rem(me, 2) + lax.rem(m, 2), 2)

    def load(f):
        return pltpu.make_async_copy(
            volt.at[:, f * frame : (f + 1) * frame], vp.at[f + past], load_sem.at[f]
        )

    order = list(range(1, n_frames)) + [0]
    for f in order:
        load(f).start()
    barrier = pltpu.get_barrier_semaphore()
    for o in range(1, n_feed):
        pl.semaphore_signal(barrier, inc=1, device_id={"feed": lax.rem(me + o, n_feed)}, device_id_type=MESH)
    for o in range(1, n_time):
        pl.semaphore_signal(barrier, inc=1, device_id={"tm": lax.rem(tm + o, n_time)}, device_id_type=MESH)

    for k in range(frame // 128):
        value = trig[:, 256 + k : 257 + k] * trig[:, :128]
        value = value - trig[:, 256 + frame // 128 + k : 257 + frame // 128 + k] * trig[:, 128:256]
        coeffs[:, k * 128 : (k + 1) * 128] = (value * (1.0 / math.sqrt(frame))).astype(jnp.bfloat16)

    def spectra(f):
        width = 256

        def chunk(c, _):
            lanes = pl.ds(pl.multiple_of(c * width, width), width)
            total = window[0:1, lanes] * vp[f, :, lanes].astype(jnp.float32)
            for t in range(1, TAPS):
                total = total + window[t : t + 1, lanes] * vp[f + t, :, lanes].astype(jnp.float32)
            filt[:, lanes] = total.astype(jnp.bfloat16)
            return 0

        lax.fori_loop(0, frame // width, chunk, 0)
        return lax.dot_general(coeffs[...], filt[...], NT, preferred_element_type=jnp.float32)

    def hist_copy(to):
        return pltpu.make_async_remote_copy(
            src_ref=hist_out, dst_ref=hist_in, send_sem=hist_sem.at[0], recv_sem=hist_sem.at[1],
            device_id={"tm": to}, device_id_type=MESH,
        )

    def send_copy(q, m):
        to = partner(m)
        return pltpu.make_async_remote_copy(
            src_ref=send.at[q, to], dst_ref=recv.at[me, q],
            send_sem=send_sem.at[q, m], recv_sem=recv_sem.at[q, m],
            device_id={"feed": to}, device_id_type=MESH,
        )

    def arrival(q, m):
        back = partner(m)
        return pltpu.make_async_remote_copy(
            src_ref=send.at[q, back], dst_ref=recv.at[back, q],
            send_sem=send_sem.at[q, m], recv_sem=recv_sem.at[q, m],
            device_id={"feed": back}, device_id_type=MESH,
        )

    def own_copy(q):
        return pltpu.make_async_copy(send.at[q, me], recv.at[me, q], own_sem.at[q])

    def far_first(k):
        return lax.rem(k + n_feed // 2 - 1, n_feed - 1) + 1

    lower = lax.broadcasted_iota(jnp.int32, (8, inputs), 0) < 4

    def quad(q, first):
        def one(k, _):
            value = spectra(q * 4 + k)
            if first:
                value = value + jnp.where(k < past, 1.0, 0.0) * hist_in[jnp.minimum(k, past - 1)].astype(jnp.float32)
            tmp[k] = value
            return 0

        lax.fori_loop(0, 4, one, 0)

        def pack(d, _):
            parts = [[], []]
            at = pl.multiple_of(d * 24, 8)
            for pair in range(2):
                a0, b0, c0 = (tmp[2 * pair, pl.ds(at + 8 * k, 8)] for k in range(3))
                a1, b1, c1 = (tmp[2 * pair + 1, pl.ds(at + 8 * k, 8)] for k in range(3))
                parts[0] += [a0, a1, jnp.where(lower, b0, pltpu.roll(b1, 4, 0))]
                parts[1] += [c0, c1, jnp.where(lower, pltpu.roll(b0, 4, 0), b1)]
            send[q, d, 0] = jnp.concatenate(parts[0], axis=0).astype(jnp.bfloat16)
            send[q, d, 1] = jnp.concatenate(parts[1], axis=0).astype(jnp.bfloat16)
            return 0

        lax.fori_loop(0, n_feed, pack, 0)

        if q == 1:
            pl.semaphore_wait(barrier, n_feed - 1 + n_time - 1)

        def start(k, _):
            send_copy(q, far_first(k)).start()
            return 0

        lax.fori_loop(0, n_feed - 1, start, 0)
        own_copy(q).start()

    def tail_frames():
        def tail_frame(k, _):
            hist_out[k] = spectra(n_frames + k).astype(jnp.bfloat16)
            return 0

        lax.fori_loop(0, past, tail_frame, 0)

        @pl.when(tm < n_time - 1)
        def _():
            hist_copy(lax.rem(tm + 1, n_time)).start()

    for f in range(1, 8):
        load(f).wait()
    quad(1, False)
    for t in range(past):
        vp[t] = jnp.zeros_like(vp[t])
        vp[n_frames + past + t] = jnp.zeros_like(vp[t])
    for q in range(2, quads):
        for f in range(4 * q, 4 * q + 4):
            load(f).wait()
        if q == quads - 1:
            tail_frames()
        quad(q, False)
    load(0).wait()

    @pl.when(tm > 0)
    def _():
        hist_copy(lax.rem(tm + n_time - 1, n_time)).wait_recv()

    @pl.when(tm == 0)
    def _():
        hist_in[...] = jnp.zeros_like(hist_in)

    quad(0, True)

    total = n_feed * inputs
    which = lax.broadcasted_iota(jnp.int32, (total, inputs), 0)

    def ones(s, _):
        onehot[s] = jnp.where(which == slots[s], 1.0, 0.0).astype(jnp.bfloat16)
        return 0

    lax.fori_loop(0, n_feed, ones, 0)

    step = 512

    def place(s, lo, hi, fresh):
        count = hi - lo
        block = recv[s, lo:hi].reshape(count * 96, inputs)

        def part(n, _):
            at = pl.multiple_of(n * step, step)
            got = lax.dot_general(block, onehot[s, pl.ds(at, step), :], NT, preferred_element_type=jnp.float32)
            got = got.reshape(count, 2, 48, step)
            if fresh:
                acc[lo:hi, :, :, pl.ds(at, step)] = got
            else:
                acc[lo:hi, :, :, pl.ds(at, step)] += got
            return 0

        lax.fori_loop(0, total // step, part, 0)

    def gather(lo, hi):
        for q in range(lo, hi):
            own_copy(q).wait()
        place(me, lo, hi, True)

        def source(k, _):
            for q in range(lo, hi):
                arrival(q, k + 1).wait_recv()
            place(partner(k + 1), lo, hi, False)
            return 0

        lax.fori_loop(0, n_feed - 1, source, 0)

    def beamform(lo, hi):
        count = hi - lo

        def cells(part, at):
            return acc[lo:hi, part, :, at : at + NS].reshape(count * 48, NS).astype(jnp.bfloat16)

        stacked = [jnp.concatenate([cells(part, g * NS) for g in range(2 * CYL)], axis=0) for part in range(2)]
        value = jnp.dot(stacked[0], t1[...], preferred_element_type=jnp.float32)
        value = value + jnp.dot(stacked[1], t2[...], preferred_element_type=jnp.float32)
        for p in range(2):
            z = []
            for y in range(CYL):
                one = value[(p * CYL + y) * count * 48 : (p * CYL + y + 1) * count * 48]
                z.append((one[:, :NS], one[:, NS:]))
            (r0, i0), (r1, i1), (r2, i2), (r3, i3) = z
            t0r, t1r, t2r, t3r = r0 + r2, r0 - r2, r1 + r3, r1 - r3
            t0i, t1i, t2i, t3i = i0 + i2, i0 - i2, i1 + i3, i1 - i3
            re = [t0r + t2r, t1r + t3i, t0r - t2r, t1r - t3i]
            im = [t0i + t2i, t1i - t3r, t0i - t2i, t1i + t3r]
            for e in range(CYL):
                at = (p * CYL + e) * NS
                for part, beam in ((0, re[e]), (1, im[e])):
                    beams[part, lo:hi, :, at : at + NS] = (beam * 0.5).astype(jnp.bfloat16).reshape(count, 48, NS)

    gather(1, quads)
    beamform(1, quads)
    gather(0, 1)
    beamform(0, 1)

    def power_copy(o, e):
        to = lax.rem(tm + o, n_time)
        return pltpu.make_async_remote_copy(
            src_ref=psend.at[e, to], dst_ref=precv.at[o - 1, e],
            send_sem=psend_sem.at[o - 1, e], recv_sem=precv_sem.at[o - 1, e],
            device_id={"tm": to}, device_id_type=MESH,
        )

    outs = upm.shape[0] // 2
    for e in range(CYL):
        summed = 0.0
        for p in range(2):
            at = (p * CYL + e) * NS
            up = jnp.dot(upm[...], beams[:, :, :, at : at + NS].reshape(-1, NS), preferred_element_type=jnp.float32)
            summed = summed + up[:outs] * up[:outs] + up[outs:] * up[outs:]
        summed = (summed * scale).reshape(n_time, own_rows, NS)
        power[e] = summed
        psend[e] = summed.astype(jnp.bfloat16)
        for o in range(1, n_time):
            power_copy(o, e).start()
    for e in range(CYL):
        result = power[e, tm]
        for o in range(1, n_time):
            power_copy(o, e).wait_recv()
            result = result + precv[o - 1, e].astype(jnp.float32)
        out[:, e * NS : (e + 1) * NS] = result
    for e in range(CYL):
        for o in range(1, n_time):
            power_copy(o, e).wait_send()

    def drain(k, _):
        for q in range(quads):
            send_copy(q, k + 1).wait_send()
        return 0

    lax.fori_loop(0, n_feed - 1, drain, 0)

    @pl.when(tm < n_time - 1)
    def _():
        hist_copy(lax.rem(tm + 1, n_time)).wait_send()


def row_order(quads):
    frames, chans = [], []
    for q in range(quads):
        for pair in range(2):
            f = 4 * q + 2 * pair
            frames += [f] * 8 + [f + 1] * 8 + [f] * 4 + [f + 1] * 4
            chans += list(range(8)) * 2 + list(range(8, 12)) * 2
    return np.array(frames), np.array(chans)


def rounded_pair(modulus, first, second):
    angle = (first[:, None] * second[None, :] % modulus) * (2.0 * np.pi / modulus)
    scale = 1.0 / np.sqrt(modulus)
    bf16 = jnp.bfloat16
    return (
        (np.cos(angle) * scale).astype(np.float32).astype(bf16),
        (np.sin(angle) * scale).astype(np.float32).astype(bf16),
    )


def window_table():
    length = TAPS * 2 * CHANNELS
    sample = np.arange(length)
    offset = (sample - length / 2 + 0.5) / (2 * CHANNELS)
    taper = 0.5 - 0.5 * np.cos(2.0 * np.pi * (sample + 0.5) / length)
    return (np.sinc(offset) * taper).astype(np.float32).reshape(TAPS, 2 * CHANNELS)


def local_fused(voltages, feed_slot, channel_flags):
    bf16 = jnp.bfloat16
    frame = 2 * CHANNELS
    inputs = voltages.shape[0]
    n_frames = voltages.shape[1] // frame
    n_time = lax.axis_size("tm")
    n_feed = lax.axis_size("feed")
    chans = LIVE_DEV * n_time
    quads = n_frames // 4
    live = live_channels(channel_flags, chans * n_feed).reshape(n_feed, chans)
    row_chan = jnp.concatenate([live, live[:, 8:], live[:, :8]], axis=1).reshape(-1)
    quarter = frame // 4
    shift = np.tile(np.where(np.arange(2 * chans) >= chans, quarter, 0), n_feed)
    fine = np.arange(128)
    coarse = np.arange(frame // 128) * 128
    step = jnp.array(np.concatenate([fine, fine, coarse, coarse]), jnp.int32)
    lag = np.concatenate([fine * 0, fine * 0 + quarter, coarse * 0, coarse * 0 + quarter])
    turned = np.concatenate([fine * 0, fine * 0, coarse * 0 + 1, coarse * 0 + 1])
    extra = jnp.array(shift[:, None] * turned[None, :] + frame - lag[None, :], jnp.int32)
    product = (row_chan[:, None] * step[None, :] + extra) & (frame - 1)
    trig = jnp.cos(product.astype(jnp.float32) * (2.0 * jnp.pi / frame))
    index = np.arange(NS)
    c, d = rounded_pair(NS, index, index)
    t1 = jnp.array(np.concatenate([c, -d], axis=1))
    t2 = jnp.array(np.concatenate([d, c], axis=1))
    frames, row_ch = row_order(quads)
    up_cos, up_sin = rounded_pair(UPCH, np.arange(UPCH), frames)
    same = (np.arange(chans)[:, None] == row_ch[None, :])[:, None, :].astype(np.float32)
    cm = (same * up_cos.astype(np.float32)[None]).reshape(chans * UPCH, -1)
    sm = (same * up_sin.astype(np.float32)[None]).reshape(chans * UPCH, -1)
    upm = np.concatenate([np.concatenate([cm, sm], 1), np.concatenate([-sm, cm], 1)], 0)
    upm = jnp.array(upm.astype(bf16))
    rows = 2 * chans * n_feed
    total = n_feed * inputs
    own_rows = LIVE_DEV * UPCH
    vmem = pl.BlockSpec(memory_space=pltpu.VMEM)
    dma = pltpu.SemaphoreType.DMA
    result = pl.pallas_call(
        functools.partial(fused_kernel, n_feed, n_time, n_frames, 1.0 / (2.0 * n_time)),
        out_shape=jax.ShapeDtypeStruct((own_rows, CYL * NS), jnp.float32),
        in_specs=[pl.BlockSpec(memory_space=pl.ANY)] + [vmem] * 6,
        out_specs=vmem,
        scratch_shapes=[
            pltpu.VMEM((n_frames + 2 * TAPS - 2, inputs, frame), bf16),
            pltpu.VMEM((rows, frame), bf16),
            pltpu.VMEM((inputs, frame), bf16),
            pltpu.VMEM((4, rows, inputs), jnp.float32),
            pltpu.VMEM((quads, n_feed, 2, 48, inputs), bf16),
            pltpu.VMEM((n_feed, quads, 2, 48, inputs), bf16),
            pltpu.VMEM((TAPS - 1, rows, inputs), bf16),
            pltpu.VMEM((TAPS - 1, rows, inputs), bf16),
            pltpu.VMEM((n_feed, total, inputs), bf16),
            pltpu.VMEM((quads, 2, 48, total), jnp.float32),
            pltpu.VMEM((2, quads, 48, total), bf16),
            pltpu.VMEM((CYL, n_time, own_rows, NS), jnp.float32),
            pltpu.VMEM((CYL, n_time, own_rows, NS), bf16),
            pltpu.VMEM((n_time - 1, CYL, own_rows, NS), bf16),
            dma((n_frames,)),
            dma((quads,)),
            dma((2,)),
            dma((quads, n_feed)),
            dma((quads, n_feed)),
            dma((n_time - 1, CYL)),
            dma((n_time - 1, CYL)),
        ],
        compiler_params=pltpu.CompilerParams(
            collective_id=0, has_side_effects=True, vmem_limit_bytes=62 * 1024 * 1024
        ),
    )(voltages, trig, jnp.array(window_table()), feed_slot.reshape(n_feed, 1, inputs), t1, t2, upm)
    return result.reshape(LIVE_DEV, UPCH, CYL * NS)


def local(voltages, feed_slot, channel_flags):
    fits = (
        voltages.shape[0] == NS
        and voltages.shape[1] == UPCH * 2 * CHANNELS
        and lax.axis_size("tm") == 4
        and lax.axis_size("feed") == 8
        and lax.axis_size("feed") * voltages.shape[0] == 2 * CYL * NS
    )
    return (local_fused if fits else local_plain)(voltages, feed_slot, channel_flags)


def solution(mesh):
    in_specs = (P("feed", "tm"), P(), P())
    out_specs = P(("feed", "tm"), None, None)
    return jax.shard_map(local, mesh=mesh, in_specs=in_specs, out_specs=out_specs, check_vma=False)
```
